32 devices in a mesh: seq: 16 (over z, x, core), tp: 2 (over y).
Axes of the slice: x: 2, y: 2, z: 4, core: 2. Of those that a mesh axis runs over, the one named last changes fastest.
Arguments:
- hidden: bfloat16 [8192, 4096], P('seq', 'tp'), may hold values from -6 to 6
- w_query: bfloat16 [4096, 4096], P(None, 'tp'), may hold values from -0.09375 to 0.09375
- w_key: bfloat16 [4096, 1024], P(None, 'tp'), may hold values from -0.09375 to 0.09375
- w_value: bfloat16 [4096, 1024], P(None, 'tp'), may hold values from -0.09375 to 0.09375
- w_out: bfloat16 [4096, 4096], P('tp'), may hold values from -0.09375 to 0.09375
- cache_keys: bfloat16 [256, 64, 1024], P('seq', None, 'tp'), may hold values from -52 to 52
- cache_values: bfloat16 [256, 64, 1024], P('seq', None, 'tp'), may hold values from -6 to 6
- cached_len: int32 [16], replicated, may hold values from 0 to 2048, as said below
- page_table: int32 [256, 2], P('seq'), may hold values from 0 to 31, as said below
Outputs:
- attn_out: bfloat16 [8192, 4096], P('seq', 'tp')
The draws below stay inside these ranges and needn't reach their ends.
Inputs may be any that keep to these rules, and one draw needn't show every extreme that they name: `cached_len`: cached tokens of each request; some request has exactly 2048. `page_table`: row b is (r, j): pool block b holds request r's cached positions j * 64 to j * 64 + 63. Request r owns exactly ceil(cached_len[r] / 64) blocks, with places 0 to that count - 1, each once; every pool block is owned; the 16 blocks of one index of seq hold at most 2 blocks of any one request, and some index holds exactly 2 of some request.
All inputs are finite; a program needn't handle non-finite values.
Results may differ from the reference program's by a relative error of at most 0.019.
Values may be sent and summed in bfloat16 or wider, within the bound.
No kernel may reach another device: no remote copies, remote signals or barrier semaphores. Data moves between devices by JAX's collectives and lax.ppermute only.
A program may use at most 256 MiB of HBM per device.

```python
import math
import jax
import jax.numpy as jnp
from jax import lax

D = 4096
HEADS = 32
KV_HEADS = 8
HD = 128
NEW = 512
CTX = 2048
BLK = 64
TOKENS = 8192
REQS = 16
NBLK_DEV = 16
NBLK_TOTAL = 256


def pool_layout(key):
    key_pairs, key_offset, key_order, key_spread = jax.random.split(jax.random.fold_in(key, 7), 4)
    places = CTX // BLK
    half_count = REQS // 2
    first = jax.random.randint(key_pairs, (half_count,), 0, places + 1).astype(jnp.int32)
    first = first.at[0].set(places)
    counts = jnp.concatenate([first, places - first])
    offset = jax.random.randint(key_offset, (REQS,), 0, BLK).astype(jnp.int32)
    offset = offset.at[0].set(0)
    lengths = jnp.maximum(counts * BLK - offset, 0)
    order = jax.random.permutation(key_order, REQS)
    lengths = lengths[order]
    counts = counts[order]
    ends = jnp.cumsum(counts)
    starts = ends - counts
    block_ids = jnp.arange(NBLK_TOTAL, dtype=jnp.int32)
    owners = jnp.sum((block_ids[:, None] >= ends[None, :]).astype(jnp.int32), axis=1)
    owners = jnp.minimum(owners, REQS - 1)
    place = block_ids - starts[owners]
    holders = NBLK_TOTAL // NBLK_DEV
    spread = jax.random.permutation(key_spread, holders).astype(jnp.int32)
    rows = spread[block_ids % holders] * NBLK_DEV + block_ids // holders
    table = jnp.zeros((NBLK_TOTAL, 2), jnp.int32).at[rows].set(jnp.stack([owners, place], axis=1))
    return (lengths.astype(jnp.int32), table)


def draw_cached_len(key, part):
    return pool_layout(key)[0]


def draw_page_table(key, part):
    return pool_layout(key)[1]


def draw_cache_keys(key, part):
    key_main = jax.random.fold_in(jax.random.fold_in(key, 11), 0)
    shape = (NBLK_TOTAL, BLK, KV_HEADS * HD)
    values = jnp.clip(jax.random.normal(key_main, shape, jnp.float32), -6.0, 6.0)
    return values.astype(jnp.bfloat16)


def block_scale(stream_key, dims, cuts, low, high):
    level = 1.0
    for dim, parts in cuts:
        steps = jax.random.uniform(jax.random.fold_in(jax.random.fold_in(stream_key, 6), dim), (parts,), jnp.float32, low / len(cuts), high / len(cuts))
        level = level * jnp.repeat(jnp.exp(steps), dims[dim] // parts).reshape((-1,) + (1,) * (len(dims) - 1 - dim))
    return level


def gaussian(own_key, extent, scale, limit, shards=(), kind=jnp.bfloat16):
    values = scale * jax.random.normal(own_key, extent, jnp.float32)
    if shards:
        values = values * block_scale(own_key, extent, shards, -0.22, 0.18)
    return jnp.clip(values, -limit, limit).astype(kind)


def setup_inputs(seed: int = 0) -> dict:
    key_list = jax.random.split(jax.random.key(seed), 10)
    hidden = gaussian(key_list[0], (TOKENS, D), 1.0, 6.0, ((0, 16), (1, 2)))
    w_query = gaussian(key_list[1], (D, HEADS * HD), D ** -0.5, 0.09375, ((1, 2),))
    w_key = gaussian(key_list[2], (D, KV_HEADS * HD), D ** -0.5, 0.09375, ((1, 2),))
    w_value = gaussian(key_list[3], (D, KV_HEADS * HD), D ** -0.5, 0.09375, ((1, 2),))
    w_out = gaussian(key_list[4], (HEADS * HD, D), (HEADS * HD) ** -0.5, 0.09375, ((0, 2),))
    cache_keys = draw_cache_keys(jax.random.fold_in(key_list[9], 71), 0)
    cache_values = gaussian(key_list[6], (NBLK_TOTAL, BLK, KV_HEADS * HD), 1.0, 6.0, ((0, 16), (2, 2)))
    cached_len = draw_cached_len(jax.random.fold_in(key_list[9], 71), 0)
    page_table = draw_page_table(jax.random.fold_in(key_list[9], 71), 0)
    return dict(hidden=hidden, w_query=w_query, w_key=w_key, w_value=w_value, w_out=w_out, cache_keys=cache_keys, cache_values=cache_values, cached_len=cached_len, page_table=page_table)


ROPE_BASE = 1000000.0
masked_score = -1e+30

def norm_rope(values, positions):
    values = values * lax.rsqrt(lax.optimization_barrier(jnp.mean(values * values, axis=-1, keepdims=True)) + 1e-06)
    half_width = values.shape[-1] // 2
    freqs = jnp.exp(jnp.arange(half_width, dtype=jnp.float32) * (-2.0 * math.log(ROPE_BASE) / values.shape[-1]))
    angles = positions.astype(jnp.float32)[:, None] * freqs[None, :]
    cosine = jnp.cos(angles)[:, None, :]
    sine = jnp.sin(angles)[:, None, :]
    first = values[..., :half_width]
    second = values[..., half_width:]
    return jnp.concatenate([first * cosine - second * sine, second * cosine + first * sine], axis=-1)

def reference(hidden, w_query, w_key, w_value, w_out, cache_keys, cache_values, cached_len, page_table):
    group = HEADS // KV_HEADS
    query_all = jnp.dot(hidden, w_query, preferred_element_type=jnp.float32).reshape(TOKENS, HEADS, HD)
    key_all = jnp.dot(hidden, w_key, preferred_element_type=jnp.float32).reshape(TOKENS, KV_HEADS, HD)
    value_all = jnp.dot(hidden, w_value, preferred_element_type=jnp.float32).reshape(TOKENS, KV_HEADS, HD)
    token_index = jnp.arange(TOKENS, dtype=jnp.int32)
    positions = cached_len[token_index // NEW] + token_index % NEW
    queries = norm_rope(query_all, positions).astype(jnp.bfloat16)
    new_keys = norm_rope(key_all, positions).astype(jnp.bfloat16)
    new_values = value_all.astype(jnp.bfloat16)
    places = CTX // BLK
    lookup = jnp.zeros((REQS, places), jnp.int32).at[page_table[:, 0], page_table[:, 1]].set(jnp.arange(NBLK_TOTAL, dtype=jnp.int32))

    def one_request(request):
        start = (request * NEW).astype(jnp.int32)
        q_here = lax.dynamic_slice_in_dim(queries, start, NEW, 0)
        k_here = lax.dynamic_slice_in_dim(new_keys, start, NEW, 0)
        v_here = lax.dynamic_slice_in_dim(new_values, start, NEW, 0)
        slots = lookup[request]
        cached_k = cache_keys[slots].reshape(CTX, KV_HEADS, HD)
        cached_v = cache_values[slots].reshape(CTX, KV_HEADS, HD)
        keys = jnp.concatenate([cached_k, k_here], axis=0).astype(jnp.float32)
        values = jnp.concatenate([cached_v, v_here], axis=0).astype(jnp.float32)
        length = cached_len[request]
        cache_ok = jnp.arange(CTX, dtype=jnp.int32) < length
        own = jnp.arange(NEW, dtype=jnp.int32)
        fresh_ok = own[None, :] <= own[:, None]
        valid = jnp.concatenate([jnp.broadcast_to(cache_ok[None, :], (NEW, CTX)), fresh_ok], axis=1)
        grouped = q_here.astype(jnp.float32).reshape(NEW, KV_HEADS, group, HD)
        scores = jnp.einsum('ikgd,jkd->kgij', grouped, keys) * HD ** (-0.5)
        scores = jnp.where(valid[None, None], scores, masked_score)
        top = lax.optimization_barrier(jnp.max(scores, axis=-1, keepdims=True))
        weights = jnp.exp(scores - top)
        total = lax.optimization_barrier(jnp.sum(weights, axis=-1))
        rounded = lax.optimization_barrier(weights.astype(jnp.bfloat16)).astype(jnp.float32)
        mixed = jnp.einsum('kgij,jkd->ikgd', rounded, values) / jnp.transpose(total, (2, 0, 1))[..., None]
        return mixed.reshape(NEW, HEADS * HD).astype(jnp.bfloat16)
    attended = lax.map(one_request, jnp.arange(REQS, dtype=jnp.int32)).reshape(TOKENS, HEADS * HD)
    return jnp.dot(attended, w_out, preferred_element_type=jnp.float32).astype(jnp.bfloat16)
```

```python
import math

import jax
import jax.numpy as jnp
from jax import lax
from jax.experimental import pallas as pl
from jax.experimental.pallas import tpu as pltpu
from jax.sharding import PartitionSpec as P

HD = 128
NEW = 512
CTX = 2048
ROPE_BASE = 1000000.0
masked_score = -1e30
VMEM_LIMIT = 56 * 1024 * 1024
BF16 = jnp.bfloat16
F32 = jnp.float32


def params(count):
    return pltpu.CompilerParams(
        dimension_semantics=("arbitrary",) * count, vmem_limit_bytes=VMEM_LIMIT
    )


def pick_blocks(page_table, cache_keys, cache_values, head, seq, per_peer):
    blocks, block_len, _ = cache_keys.shape

    def body(table, keys, values, out, index, sem):
        for slot in range(seq * per_peer):
            index[slot] = 0
        counts = index.at[pl.ds(seq * per_peer, seq)]
        for r in range(seq):
            counts[r] = 0

        def place(b, carry):
            request = table[b, 0]
            taken = counts[request]
            index[request * per_peer + jnp.minimum(taken, per_peer - 1)] = b
            counts[request] = taken + 1
            return carry

        lax.fori_loop(0, blocks, place, 0)
        for r in range(seq):
            for k in range(per_peer):
                b = index[r * per_peer + k]
                for which, source in enumerate((keys, values)):
                    pltpu.make_async_copy(
                        source.at[b, :, pl.ds(head * HD, HD)],
                        out.at[r, which, pl.ds(k * block_len, block_len), :],
                        sem,
                    ).start()
        pltpu.make_async_copy(out, out, sem).wait()

    return pl.pallas_call(
        body,
        in_specs=[
            pl.BlockSpec(memory_space=pltpu.SMEM),
            pl.BlockSpec(memory_space=pl.ANY),
            pl.BlockSpec(memory_space=pl.ANY),
        ],
        out_specs=pl.BlockSpec(memory_space=pl.ANY),
        out_shape=jax.ShapeDtypeStruct((seq, 2, per_peer * block_len, HD), BF16),
        scratch_shapes=[pltpu.SMEM((seq * per_peer + seq,), jnp.int32), pltpu.SemaphoreType.DMA],
        name="pick_blocks",
    )(page_table, cache_keys, cache_values)


def project_own(row_block, x, weight):
    tokens, depth = x.shape
    width = weight.shape[1]
    step = min(512, width)

    def body(rows, x_ref, w_ref, o_ref):
        o_ref[...] = jnp.dot(x_ref[...], w_ref[...], preferred_element_type=F32)

    return pl.pallas_call(
        body,
        grid_spec=pltpu.PrefetchScalarGridSpec(
            num_scalar_prefetch=1,
            grid=(width // step,),
            in_specs=[
                pl.BlockSpec((tokens, depth), lambda n, rows: (0, 0)),
                pl.BlockSpec((depth, step), lambda n, rows: (rows[0], n)),
            ],
            out_specs=pl.BlockSpec((tokens, step), lambda n, rows: (0, n)),
        ),
        out_shape=jax.ShapeDtypeStruct((tokens, width), F32),
        compiler_params=params(1),
        name="project_own",
    )(row_block, x, weight)


def project_rest(row_blocks, pieces, weight, partial, cosine, sine, scale):
    tokens, depth = pieces[0].shape
    count = len(pieces)
    width = weight.shape[1]
    step = min(512, width)
    heads = step // HD

    def body(rows, *refs):
        x_refs = refs[:count]
        w_refs = refs[count : 2 * count]
        p_ref, c_ref, s_ref, o_ref = refs[2 * count :]
        total = p_ref[...]
        for x_ref, w_ref in zip(x_refs, w_refs):
            total = total + jnp.dot(x_ref[...], w_ref[...], preferred_element_type=F32)
        for h in range(heads):
            u = total[:, h * HD : (h + 1) * HD]
            if scale is not None:
                inverse = lax.rsqrt(jnp.mean(u * u, axis=-1, keepdims=True) + 1e-06) * scale
                u = u * inverse
                u = u * c_ref[...] + pltpu.roll(u, HD // 2, 1) * s_ref[...]
            o_ref[h] = u.astype(BF16)

    def weight_spec(i):
        return pl.BlockSpec((depth, step), lambda n, rows: (rows[i], n))

    return pl.pallas_call(
        body,
        grid_spec=pltpu.PrefetchScalarGridSpec(
            num_scalar_prefetch=1,
            grid=(width // step,),
            in_specs=[pl.BlockSpec((tokens, depth), lambda n, rows: (0, 0))] * count
            + [weight_spec(i) for i in range(count)]
            + [
                pl.BlockSpec((tokens, step), lambda n, rows: (0, n)),
                pl.BlockSpec((tokens, HD), lambda n, rows: (0, 0)),
                pl.BlockSpec((tokens, HD), lambda n, rows: (0, 0)),
            ],
            out_specs=pl.BlockSpec((heads, tokens, HD), lambda n, rows: (n, 0, 0)),
        ),
        out_shape=jax.ShapeDtypeStruct((width // HD, tokens, HD), BF16),
        compiler_params=params(1),
        name="project_rest",
    )(row_blocks, *pieces, *([weight] * count), partial, cosine, sine)


def attend(head, queries, fresh_keys, fresh_values, cached, bias, attended, group):
    heads, tokens, _ = queries.shape
    sources, _, rows, _ = cached.shape
    keys_count = sources * rows

    def body(q_ref, fk_ref, fv_ref, c_ref, b_ref, *rest):
        o_ref = rest[-1]
        q = q_ref[0]
        cached_keys = c_ref[:, 0].reshape(keys_count, HD)
        cached_values = c_ref[:, 1].reshape(keys_count, HD)
        contract = (((1,), (1,)), ((), ()))
        old = lax.dot_general(q, cached_keys, contract, preferred_element_type=F32) + b_ref[...]
        new = lax.dot_general(q, fk_ref[0], contract, preferred_element_type=F32)
        row = lax.broadcasted_iota(jnp.int32, (tokens, tokens), 0)
        col = lax.broadcasted_iota(jnp.int32, (tokens, tokens), 1)
        new = jnp.where(col <= row, new, masked_score)
        top = jnp.maximum(jnp.max(old, axis=1, keepdims=True), jnp.max(new, axis=1, keepdims=True))
        old = jnp.exp2(old - top)
        new = jnp.exp2(new - top)
        total = jnp.sum(old, axis=1, keepdims=True) + jnp.sum(new, axis=1, keepdims=True)
        mixed = jnp.dot(old.astype(BF16), cached_values, preferred_element_type=F32)
        mixed = mixed + jnp.dot(new.astype(BF16), fv_ref[0], preferred_element_type=F32)
        o_ref[...] = (mixed / total).astype(BF16)

    in_specs = [
        pl.BlockSpec((1, tokens, HD), lambda g: (head * group + g, 0, 0)),
        pl.BlockSpec((1, tokens, HD), lambda g: (head, 0, 0)),
        pl.BlockSpec((1, tokens, HD), lambda g: (head, 0, 0)),
        pl.BlockSpec(cached.shape, lambda g: (0, 0, 0, 0)),
        pl.BlockSpec((1, keys_count), lambda g: (0, 0)),
    ]
    operands = [queries, fresh_keys, fresh_values, cached, bias]
    aliases = {}
    if attended is not None:
        in_specs.append(pl.BlockSpec(memory_space=pl.ANY))
        operands.append(attended)
        aliases = {5: 0}
    return pl.pallas_call(
        body,
        grid=(group,),
        in_specs=in_specs,
        out_specs=pl.BlockSpec((tokens, HD), lambda g: (0, head * group + g)),
        out_shape=jax.ShapeDtypeStruct((tokens, heads * HD), BF16),
        input_output_aliases=aliases,
        compiler_params=params(1),
        name="attend",
    )(*operands)


def project_out(col_block, attended, weight, width, chunk, chunks, kind):
    tokens, depth = attended.shape
    rows = tokens // chunks
    step = min(512, width)
    steps = width // step

    def body(cols, x_ref, w_ref, o_ref):
        o_ref[...] = jnp.dot(x_ref[...], w_ref[...], preferred_element_type=F32).astype(kind)

    return pl.pallas_call(
        body,
        grid_spec=pltpu.PrefetchScalarGridSpec(
            num_scalar_prefetch=1,
            grid=(steps,),
            in_specs=[
                pl.BlockSpec((rows, depth), lambda n, cols: (chunk, 0)),
                pl.BlockSpec((depth, step), lambda n, cols: (0, cols[0] * steps + n)),
            ],
            out_specs=pl.BlockSpec((rows, step), lambda n, cols: (0, n)),
        ),
        out_shape=jax.ShapeDtypeStruct((rows, width), kind),
        compiler_params=params(1),
        name="project_out",
    )(col_block, attended, weight)


def rotation(length, tokens):
    half = HD // 2
    freqs = jnp.exp(jnp.arange(half, dtype=F32) * (-2.0 * math.log(ROPE_BASE) / HD))
    positions = (length + jnp.arange(tokens, dtype=jnp.int32)).astype(F32)
    angles = positions[:, None] * freqs[None, :]
    cosine = jnp.cos(angles)
    sine = jnp.sin(angles)
    return jnp.concatenate([cosine, cosine], axis=1), jnp.concatenate([-sine, sine], axis=1)


def on_device(
    hidden, w_query, w_key, w_value, w_out, cache_keys, cache_values, cached_len, page_table
):
    tokens = hidden.shape[0]
    assert tokens == NEW
    seq = lax.axis_size("seq")
    tp = lax.axis_size("tp")
    query_heads = w_query.shape[1] // HD
    kv_heads = w_key.shape[1] // HD
    group = query_heads // kv_heads
    block_len = cache_keys.shape[1]
    per_peer = max(1, CTX // block_len // seq)
    request = lax.axis_index("seq")
    rank = lax.axis_index("tp")
    length = cached_len[request]

    received = []
    for head in range(kv_heads):
        send = pick_blocks(page_table, cache_keys, cache_values, head, seq, per_peer)
        received.append(lax.all_to_all(send, "seq", 0, 0, tiled=True))
    table = lax.all_gather(page_table[None], "seq", axis=0, tiled=True)

    pieces = []
    for shift in range(1, tp):
        pairs = [(i, (i + shift) % tp) for i in range(tp)]
        pieces.append(lax.ppermute(hidden, "tp", pairs))
    own_row = jnp.reshape(rank, (1,)).astype(jnp.int32)
    rest_rows = jnp.stack([(rank - shift) % tp for shift in range(1, tp)]).astype(jnp.int32)
    cosine, sine = rotation(length, tokens)

    def project(weight, scale):
        partial = project_own(own_row, hidden, weight)
        return project_rest(rest_rows, pieces, weight, partial, cosine, sine, scale)

    queries = project(w_query, HD ** (-0.5) / math.log(2.0))
    fresh_keys = project(w_key, 1.0)
    fresh_values = project(w_value, None)

    mine = table[..., 0] == request
    before = jnp.tril(jnp.ones((mine.shape[1], mine.shape[1]), jnp.bool_), -1)
    slot = jnp.sum(mine[:, None, :] & before[None], axis=-1)
    filled = jnp.clip(length - table[..., 1] * block_len, 0, block_len)
    slots = jnp.arange(per_peer)
    here = mine[:, None, :] & (slot[:, None, :] == slots[None, :, None])
    filled = jnp.sum(jnp.where(here, filled[:, None, :], 0), axis=-1)
    bias = jnp.where(jnp.arange(block_len) < filled[..., None], 0.0, masked_score)
    bias = bias.astype(F32).reshape(1, seq * per_peer * block_len)

    attended = None
    for head in range(kv_heads):
        attended = attend(
            head, queries, fresh_keys, fresh_values, received[head], bias, attended, group
        )

    width = w_out.shape[1] // tp
    chunks = 4 if tp == 2 else 1
    arrived = []
    for chunk in range(chunks):
        for shift in range(1, tp):
            target = jnp.reshape((rank + shift) % tp, (1,)).astype(jnp.int32)
            part = project_out(target, attended, w_out, width, chunk, chunks, BF16)
            pairs = [(i, (i + shift) % tp) for i in range(tp)]
            arrived.append(lax.ppermute(part, "tp", pairs))
    own = project_out(own_row, attended, w_out, width, 0, 1, F32)
    rows = tokens // chunks
    out = []
    for chunk in range(chunks):
        total = own[chunk * rows : (chunk + 1) * rows]
        for shift in range(1, tp):
            total = total + arrived[chunk * (tp - 1) + shift - 1].astype(F32)
        out.append(total.astype(BF16))
    return jnp.concatenate(out, axis=0)


def solution(mesh):
    in_specs = (
        P("seq", "tp"),
        P(None, "tp"),
        P(None, "tp"),
        P(None, "tp"),
        P("tp", None),
        P("seq", None, "tp"),
        P("seq", None, "tp"),
        P(),
        P("seq", None),
    )
    out_specs = P("seq", "tp")
    return jax.shard_map(
        on_device, mesh=mesh, in_specs=in_specs, out_specs=out_specs, check_vma=False
    )
```

```python
import math

import jax
import jax.numpy as jnp
from jax import lax
from jax.experimental import pallas as pl
from jax.experimental.pallas import tpu as pltpu
from jax.sharding import PartitionSpec as P

HD = 128
NEW = 512
CTX = 2048
ROPE_BASE = 1000000.0
masked_score = -1e30
VMEM_LIMIT = 56 * 1024 * 1024
BF16 = jnp.bfloat16
F32 = jnp.float32


def params(count):
    return pltpu.CompilerParams(
        dimension_semantics=("arbitrary",) * count, vmem_limit_bytes=VMEM_LIMIT
    )


def cost(flops, moved, exps=0):
    return pl.CostEstimate(flops=flops, bytes_accessed=moved, transcendentals=exps)


def pick_blocks(page_table, cached_len, cache_keys, cache_values, first, count, seq, per_peer):
    masked = first == 0
    width = count * HD
    blocks, block_len, _ = cache_keys.shape
    span = per_peer * block_len
    rows = 2 * span + (16 if masked else 0)

    def body(table, lengths, keys, values, out, index):
        for slot in range(seq * per_peer):
            index[slot] = 0
        tally = seq * per_peer
        for r in range(seq):
            index[tally + r] = 0

        def place(b, carry):
            r = table[b, 0]
            taken = index[tally + r]
            index[r * per_peer + jnp.minimum(taken, per_peer - 1)] = b
            index[tally + r] = taken + 1
            return carry

        lax.fori_loop(0, blocks, place, 0)
        lane = lax.broadcasted_iota(jnp.int32, (16, width), 1)
        for r in range(seq):
            mask = jnp.full((16, width), masked_score, F32)
            for k in range(per_peer):
                b = index[r * per_peer + k]
                out[r, k * block_len : (k + 1) * block_len, :] = keys[b]
                out[r, span + k * block_len : span + (k + 1) * block_len, :] = values[b]
                if masked:
                    filled = jnp.minimum(lengths[r] - table[b, 1] * block_len, block_len)
                    filled = jnp.where(index[tally + r] > k, filled, 0)
                    inside = (lane >= k * block_len) & (lane < k * block_len + filled)
                    mask = jnp.where(inside, 0.0, mask)
            if masked:
                out[r, 2 * span :, :] = mask.astype(BF16)

    part = pl.BlockSpec((blocks, block_len, width), lambda i: (0, 0, first // count))
    return pl.pallas_call(
        body,
        grid=(1,),
        in_specs=[
            pl.BlockSpec(memory_space=pltpu.SMEM),
            pl.BlockSpec(memory_space=pltpu.SMEM),
            part,
            part,
        ],
        out_specs=pl.BlockSpec((seq, rows, width), lambda i: (0, 0, 0)),
        out_shape=jax.ShapeDtypeStruct((seq, rows, width), BF16),
        scratch_shapes=[pltpu.SMEM((seq * per_peer + seq,), jnp.int32)],
        compiler_params=params(1),
        cost_estimate=cost(0, 2 * seq * rows * width * 2),
        name="pick_blocks",
    )(page_table, cached_len, cache_keys, cache_values)


def project_own(row_block, x, weight):
    tokens, depth = x.shape
    width = weight.shape[1]
    step = min(512, width)

    def body(rows, x_ref, w_ref, o_ref):
        o_ref[...] = jnp.dot(x_ref[...], w_ref[...], preferred_element_type=F32)

    return pl.pallas_call(
        body,
        grid_spec=pltpu.PrefetchScalarGridSpec(
            num_scalar_prefetch=1,
            grid=(width // step,),
            in_specs=[
                pl.BlockSpec((tokens, depth), lambda n, rows: (0, 0)),
                pl.BlockSpec((depth, step), lambda n, rows: (rows[0], n)),
            ],
            out_specs=pl.BlockSpec((tokens, step), lambda n, rows: (0, n)),
        ),
        out_shape=jax.ShapeDtypeStruct((tokens, width), F32),
        compiler_params=params(1),
        cost_estimate=cost(2 * tokens * depth * width, depth * width * 2 + tokens * width * 4),
        name="project_own",
    )(row_block, x, weight)


def project_rest(row_blocks, half, pieces, weight, partial, cosine, sine, scale):
    tokens, depth = pieces[0].shape
    count = len(pieces)
    width = weight.shape[1]
    step = min(512, width)
    heads = step // HD

    def body(rows, *refs):
        x_refs = refs[:count]
        w_refs = refs[count : 2 * count]
        p_ref, c_ref, s_ref, o_ref = refs[2 * count :]
        total = p_ref[...]
        for x_ref, w_ref in zip(x_refs, w_refs):
            total = total + jnp.dot(x_ref[...], w_ref[...], preferred_element_type=F32)
        for h in range(heads):
            u = total[:, h * HD : (h + 1) * HD]
            if scale is not None:
                inverse = lax.rsqrt(jnp.mean(u * u, axis=-1, keepdims=True) + 1e-06) * scale
                u = u * inverse
                u = u * c_ref[...] + pltpu.roll(u, HD // 2, 1) * s_ref[...]
            o_ref[h] = u.astype(BF16)

    def weight_spec(i):
        return pl.BlockSpec((depth, step), lambda n, rows: (rows[i], n))

    return pl.pallas_call(
        body,
        grid_spec=pltpu.PrefetchScalarGridSpec(
            num_scalar_prefetch=1,
            grid=(width // step,),
            in_specs=[pl.BlockSpec((tokens, depth), lambda n, rows: (0, 0))] * count
            + [weight_spec(i) for i in range(count)]
            + [
                pl.BlockSpec((tokens, step), lambda n, rows: (half, n)),
                pl.BlockSpec((tokens, HD), lambda n, rows: (half, 0)),
                pl.BlockSpec((tokens, HD), lambda n, rows: (half, 0)),
            ],
            out_specs=pl.BlockSpec((heads, tokens, HD), lambda n, rows: (n, 0, 0)),
        ),
        out_shape=jax.ShapeDtypeStruct((width // HD, tokens, HD), BF16),
        compiler_params=params(1),
        cost_estimate=cost(
            2 * tokens * depth * count * width, depth * count * width * 2 + tokens * width * 8
        ),
        name="project_rest",
    )(row_blocks, *pieces, *([weight] * count), partial, cosine, sine)


def attend(first, count, at, group, queries, fresh_keys, fresh_values, cached, bias, attended):
    heads, tokens, _ = queries.shape
    parts = len(fresh_keys)
    sources, all_rows, _ = cached.shape
    keys_count = bias.shape[1]
    rows = keys_count // sources
    early = tokens * (parts - 1)
    tile = 128
    contract = (((1,), (1,)), ((), ()))

    def body(*refs):
        q_ref, c_ref, b_ref = refs[:3]
        key_refs = refs[3 : 3 + parts]
        value_refs = refs[3 + parts : 3 + 2 * parts]
        o_ref, old_values, new_values = refs[-3:]

        @pl.when(pl.program_id(0) % group == 0)
        def _():
            old_values[:, :HD] = c_ref[:, rows : 2 * rows].reshape(keys_count, HD)
            old_values[:, HD:] = jnp.ones((keys_count, HD), BF16)
            for i in range(parts):
                new_values[i * tokens : (i + 1) * tokens, :HD] = value_refs[i][0]
            new_values[:, HD:] = jnp.ones((tokens * parts, HD), BF16)

        cached_keys = c_ref[:, :rows].reshape(keys_count, HD)

        def product(q, keys):
            return lax.dot_general(q, keys, contract, preferred_element_type=F32)

        def scores(t):
            q = q_ref[0, t * tile : (t + 1) * tile]
            width = (t + 1) * tile
            out = [product(q, cached_keys) + b_ref[...]]
            out += [product(q, ref[0]) for ref in key_refs[:-1]]
            row = lax.broadcasted_iota(jnp.int32, (tile, width), 0) + t * tile
            col = lax.broadcasted_iota(jnp.int32, (tile, width), 1)
            out.append(jnp.where(col <= row, product(q, key_refs[-1][0, :width]), masked_score))
            return out

        ahead = scores(0)
        for t in range(tokens // tile):
            now = ahead
            if (t + 1) * tile < tokens:
                ahead = scores(t + 1)
            top = jnp.max(now[0], axis=1, keepdims=True)
            for part in now[1:]:
                top = jnp.maximum(top, jnp.max(part, axis=1, keepdims=True))
            now = [jnp.exp2(part - top).astype(BF16) for part in now]
            mixed = jnp.dot(now[0], old_values[...], preferred_element_type=F32)
            start = 0
            for part in now[1:]:
                values = new_values[start : start + part.shape[1]]
                mixed = mixed + jnp.dot(part, values, preferred_element_type=F32)
                start += part.shape[1]
            o_ref[t * tile : (t + 1) * tile] = (mixed[:, :HD] / mixed[:, HD:]).astype(BF16)

    head_spec = pl.BlockSpec((1, tokens, HD), lambda g: (first + g // group, 0, 0))
    in_specs = [
        pl.BlockSpec((1, tokens, HD), lambda g: (first * group + g, 0, 0)),
        pl.BlockSpec((sources, all_rows, HD), lambda g: (0, 0, at + g // group)),
        pl.BlockSpec((1, keys_count), lambda g: (0, 0)),
    ] + [head_spec] * (2 * parts)
    operands = [queries, cached, bias] + list(fresh_keys) + list(fresh_values)
    aliases = {}
    if attended is not None:
        aliases = {len(operands): 0}
        in_specs.append(pl.BlockSpec(memory_space=pl.ANY))
        operands.append(attended)
    pairs = count * group * tokens * (keys_count + tokens * parts)
    return pl.pallas_call(
        body,
        grid=(count * group,),
        in_specs=in_specs,
        out_specs=pl.BlockSpec((tokens, HD), lambda g: (0, first * group + g)),
        out_shape=jax.ShapeDtypeStruct((tokens, heads * HD), BF16),
        scratch_shapes=[
            pltpu.VMEM((keys_count, 2 * HD), BF16),
            pltpu.VMEM((early + tokens, 2 * HD), BF16),
        ],
        input_output_aliases=aliases,
        compiler_params=params(1),
        cost_estimate=cost(8 * pairs * HD, 4 * count * keys_count * HD, pairs),
        name="attend",
    )(*operands)


def project_out(col_block, attended, weight, width, strips, kind):
    rows, depth = attended.shape
    strip = rows // strips
    step = min(1024, width)
    steps = width // step

    def body(cols, x_ref, w_ref, *o_refs):
        total = jnp.dot(x_ref[...], w_ref[...], preferred_element_type=F32).astype(kind)
        for i in range(strips):
            o_refs[i][...] = total[i * strip : (i + 1) * strip]

    return pl.pallas_call(
        body,
        grid_spec=pltpu.PrefetchScalarGridSpec(
            num_scalar_prefetch=1,
            grid=(steps,),
            in_specs=[
                pl.BlockSpec((rows, depth), lambda n, cols: (0, 0)),
                pl.BlockSpec((depth, step), lambda n, cols: (0, cols[0] * steps + n)),
            ],
            out_specs=[pl.BlockSpec((strip, step), lambda n, cols: (0, n))] * strips,
        ),
        out_shape=[jax.ShapeDtypeStruct((strip, width), kind)] * strips,
        compiler_params=params(1),
        cost_estimate=cost(2 * rows * depth * width, depth * width * 2 + rows * width * 4),
        name="project_out",
    )(col_block, attended, weight)


def combine(own, parts, index, total_rows, out):
    rows, width = own.shape

    def body(*refs):
        total = refs[0][...]
        for ref in refs[1 : 1 + len(parts)]:
            total = total + ref[...].astype(F32)
        refs[-1][...] = total.astype(BF16)

    step = min(1024, width)
    in_specs = [pl.BlockSpec((rows, step), lambda n: (0, n))] * (1 + len(parts))
    operands = [own] + list(parts)
    aliases = {}
    if out is not None:
        aliases = {len(operands): 0}
        in_specs.append(pl.BlockSpec(memory_space=pl.ANY))
        operands.append(out)
    return pl.pallas_call(
        body,
        grid=(width // step,),
        in_specs=in_specs,
        out_specs=pl.BlockSpec((rows, step), lambda n: (index, n)),
        out_shape=jax.ShapeDtypeStruct((total_rows, width), BF16),
        input_output_aliases=aliases,
        compiler_params=params(1),
        cost_estimate=cost(0, rows * width * 8),
        name="combine",
    )(*operands)


def rotation(length, tokens):
    half = HD // 2
    freqs = jnp.exp(jnp.arange(half, dtype=F32) * (-2.0 * math.log(ROPE_BASE) / HD))
    positions = (length + jnp.arange(tokens, dtype=jnp.int32)).astype(F32)
    angles = positions[:, None] * freqs[None, :]
    cosine = jnp.cos(angles)
    sine = jnp.sin(angles)
    return jnp.concatenate([cosine, cosine], axis=1), jnp.concatenate([-sine, sine], axis=1)


def on_device(
    hidden, w_query, w_key, w_value, w_out, cache_keys, cache_values, cached_len, page_table
):
    tokens = hidden.shape[0]
    assert tokens == NEW
    seq = lax.axis_size("seq")
    tp = lax.axis_size("tp")
    query_heads = w_query.shape[1] // HD
    kv_heads = w_key.shape[1] // HD
    group = query_heads // kv_heads
    block_len = cache_keys.shape[1]
    per_peer = max(1, CTX // block_len // seq)
    request = lax.axis_index("seq")
    rank = lax.axis_index("tp")
    length = cached_len[request]

    span = per_peer * block_len
    split = [(0, kv_heads - 1), (kv_heads - 1, 1)] if kv_heads > 1 else [(0, 1)]
    own_row = jnp.reshape(rank, (1,)).astype(jnp.int32)
    rest_rows = jnp.stack([(rank - shift) % tp for shift in range(1, tp)]).astype(jnp.int32)
    cosine, sine = rotation(length, tokens)

    def pick(first, count):
        return pick_blocks(
            page_table, cached_len, cache_keys, cache_values, first, count, seq, per_peer
        )

    def exchange(block):
        return lax.all_to_all(block, "seq", 0, 0, tiled=True)

    def swap(x, shift):
        return lax.ppermute(x, "tp", [(i, (i + shift) % tp) for i in range(tp)])

    half_tokens = tokens // 2
    received = [exchange(pick(*split[0]))]
    arrivals = []
    for half in range(2):
        mine = hidden[half * half_tokens : (half + 1) * half_tokens]
        if arrivals:
            mine, arrivals[0][0] = lax.optimization_barrier((mine, arrivals[0][0]))
        arrivals.append([swap(mine, shift) for shift in range(1, tp)])
    own_parts = [project_own(own_row, hidden, w) for w in (w_key, w_value, w_query)]

    def rest(half, parts):
        def one(weight, part, scale):
            return project_rest(
                rest_rows, half, arrivals[half], weight, part, cosine, sine, scale
            )

        return [
            one(w_key, parts[0], 1.0),
            one(w_value, parts[1], None),
            one(w_query, parts[2], HD ** (-0.5) / math.log(2.0)),
        ]

    fresh = [rest(0, own_parts), rest(1, own_parts)]
    for first, count in split[1:]:
        block, received[-1], fresh = lax.optimization_barrier(
            (pick(first, count), received[-1], fresh)
        )
        received.append(exchange(block))
    bias = received[0][:, 2 * span, :span].astype(F32).reshape(1, seq * span)
    attended = [None, None]

    def run(first, count, half):
        piece = 0 if first < split[0][1] else 1
        attended[half] = attend(
            first,
            count,
            first - split[piece][0],
            group,
            fresh[half][2],
            [fresh[i][0] for i in range(half + 1)],
            [fresh[i][1] for i in range(half + 1)],
            received[piece],
            bias,
            attended[half],
        )

    width = w_out.shape[1] // tp
    targets = [jnp.reshape((rank + s) % tp, (1,)).astype(jnp.int32) for s in range(1, tp)]
    strips = 2

    def out_parts(half):
        return [project_out(t, attended[half], w_out, width, strips, BF16) for t in targets]

    run(*split[0], 0)
    run(0, 1, 1)
    if len(split) > 1:
        received[1], attended[0], attended[1] = lax.optimization_barrier(
            (received[1], attended[0], attended[1])
        )
        run(*split[1], 0)
    other = [out_parts(0)]
    for head in range(1, kv_heads - 1):
        run(head, 1, 1)
    held = attended[1]
    if len(split) > 1:
        run(*split[1], 1)
    other.append(out_parts(1))
    own = [project_out(own_row, attended[half], w_out, width, strips, F32) for half in range(2)]
    sums = [[] for _ in range(2 * strips)]
    for shift in range(1, tp):
        for i in range(2 * strips):
            strip = other[i // strips][shift - 1][i % strips]
            if tp == 2 and i > 0:
                if i == 1:
                    strip, sums[0], held = lax.optimization_barrier((strip, sums[0], held))
                elif i == 2 * strips - 1:
                    strip, sums[i - 1], own = lax.optimization_barrier((strip, sums[i - 1], own))
                else:
                    strip, sums[i - 1] = lax.optimization_barrier((strip, sums[i - 1]))
            sums[i].append(swap(strip, shift))
    out = None
    for i in range(2 * strips):
        out = combine(own[i // strips][i % strips], sums[i], i, tokens, out)
    return out


def solution(mesh):
    in_specs = (
        P("seq", "tp"),
        P(None, "tp"),
        P(None, "tp"),
        P(None, "tp"),
        P("tp", None),
        P("seq", None, "tp"),
        P("seq", None, "tp"),
        P(),
        P("seq", None),
    )
    out_specs = P("seq", "tp")
    return jax.shard_map(
        on_device, mesh=mesh, in_specs=in_specs, out_specs=out_specs, check_vma=False
    )
```

```python
import math

import jax
import jax.numpy as jnp
from jax import lax
from jax.experimental import pallas as pl
from jax.experimental.pallas import tpu as pltpu
from jax.sharding import PartitionSpec as P

HD = 128
NEW = 512
CTX = 2048
ROPE_BASE = 1000000.0
masked_score = -1e30
VMEM_LIMIT = 56 * 1024 * 1024
BF16 = jnp.bfloat16
F32 = jnp.float32


def params(count):
    return pltpu.CompilerParams(
        dimension_semantics=("arbitrary",) * count, vmem_limit_bytes=VMEM_LIMIT
    )


def cost(flops, moved, exps=0):
    return pl.CostEstimate(flops=flops, bytes_accessed=moved, transcendentals=exps)


def pick_blocks(page_table, cached_len, cache_keys, cache_values, first, count, seq, per_peer):
    masked = first == 0
    blocks, block_len, _ = cache_keys.shape
    span = per_peer * block_len
    rows = 2 * span * count + (8 if masked else 0)
    width = count * HD

    def body(table, lengths, keys, values, out, index):
        for slot in range(seq * per_peer):
            index[slot] = 0
        tally = seq * per_peer
        for r in range(seq):
            index[tally + r] = 0

        def place(b, carry):
            r = table[b, 0]
            taken = index[tally + r]
            index[r * per_peer + jnp.minimum(taken, per_peer - 1)] = b
            index[tally + r] = taken + 1
            return carry

        lax.fori_loop(0, blocks, place, 0)
        lane = lax.broadcasted_iota(jnp.int32, (8, HD), 1)
        for r in range(seq):
            mask = jnp.full((8, HD), masked_score, F32)
            for k in range(per_peer):
                b = index[r * per_peer + k]
                for h in range(count):
                    at = 2 * h * span + k * block_len
                    columns = slice(h * HD, (h + 1) * HD)
                    out[r, at : at + block_len, :] = keys[b, :, columns]
                    out[r, at + span : at + span + block_len, :] = values[b, :, columns]
                if masked:
                    filled = jnp.minimum(lengths[r] - table[b, 1] * block_len, block_len)
                    filled = jnp.where(index[tally + r] > k, filled, 0)
                    inside = (lane >= k * block_len) & (lane < k * block_len + filled)
                    mask = jnp.where(inside, 0.0, mask)
            if masked:
                out[r, 2 * span * count :, :] = mask.astype(BF16)

    part = pl.BlockSpec((blocks, block_len, width), lambda i: (0, 0, first // count))
    return pl.pallas_call(
        body,
        grid=(1,),
        in_specs=[
            pl.BlockSpec(memory_space=pltpu.SMEM),
            pl.BlockSpec(memory_space=pltpu.SMEM),
            part,
            part,
        ],
        out_specs=pl.BlockSpec((seq, rows, HD), lambda i: (0, 0, 0)),
        out_shape=jax.ShapeDtypeStruct((seq, rows, HD), BF16),
        scratch_shapes=[pltpu.SMEM((seq * per_peer + seq,), jnp.int32)],
        compiler_params=params(1),
        cost_estimate=cost(0, 2 * seq * rows * HD * 2),
        name="pick_blocks",
    )(page_table, cached_len, cache_keys, cache_values)


def project_own(row_block, x, weight):
    tokens, depth = x.shape
    width = weight.shape[1]
    step = min(512, width)

    def body(rows, x_ref, w_ref, o_ref):
        o_ref[...] = jnp.dot(x_ref[...], w_ref[...], preferred_element_type=F32)

    return pl.pallas_call(
        body,
        grid_spec=pltpu.PrefetchScalarGridSpec(
            num_scalar_prefetch=1,
            grid=(width // step,),
            in_specs=[
                pl.BlockSpec((tokens, depth), lambda n, rows: (0, 0)),
                pl.BlockSpec((depth, step), lambda n, rows: (rows[0], n)),
            ],
            out_specs=pl.BlockSpec((tokens, step), lambda n, rows: (0, n)),
        ),
        out_shape=jax.ShapeDtypeStruct((tokens, width), F32),
        compiler_params=params(1),
        cost_estimate=cost(2 * tokens * depth * width, depth * width * 2 + tokens * width * 4),
        name="project_own",
    )(row_block, x, weight)


def project_rest(row_blocks, half, pieces, weight, partial, cosine, sine, scale):
    tokens, depth = pieces[0].shape
    count = len(pieces)
    width = weight.shape[1]
    step = min(512, width)
    heads = step // HD

    def body(rows, *refs):
        x_refs = refs[:count]
        w_refs = refs[count : 2 * count]
        p_ref, c_ref, s_ref, o_ref = refs[2 * count :]
        total = p_ref[...]
        for x_ref, w_ref in zip(x_refs, w_refs):
            total = total + jnp.dot(x_ref[...], w_ref[...], preferred_element_type=F32)
        for h in range(heads):
            u = total[:, h * HD : (h + 1) * HD]
            if scale is not None:
                inverse = lax.rsqrt(jnp.mean(u * u, axis=-1, keepdims=True) + 1e-06) * scale
                u = u * inverse
                u = u * c_ref[...] + pltpu.roll(u, HD // 2, 1) * s_ref[...]
            o_ref[h] = u.astype(BF16)

    def weight_spec(i):
        return pl.BlockSpec((depth, step), lambda n, rows: (rows[i], n))

    return pl.pallas_call(
        body,
        grid_spec=pltpu.PrefetchScalarGridSpec(
            num_scalar_prefetch=1,
            grid=(width // step,),
            in_specs=[pl.BlockSpec((tokens, depth), lambda n, rows: (0, 0))] * count
            + [weight_spec(i) for i in range(count)]
            + [
                pl.BlockSpec((tokens, step), lambda n, rows: (half, n)),
                pl.BlockSpec((tokens, HD), lambda n, rows: (half, 0)),
                pl.BlockSpec((tokens, HD), lambda n, rows: (half, 0)),
            ],
            out_specs=pl.BlockSpec((heads, tokens, HD), lambda n, rows: (n, 0, 0)),
        ),
        out_shape=jax.ShapeDtypeStruct((width // HD, tokens, HD), BF16),
        compiler_params=params(1),
        cost_estimate=cost(
            2 * tokens * depth * count * width, depth * count * width * 2 + tokens * width * 8
        ),
        name="project_rest",
    )(row_blocks, *pieces, *([weight] * count), partial, cosine, sine)


def attend(first, count, at, group, queries, fresh_keys, fresh_values, cached, bias, attended):
    heads, tokens, _ = queries.shape
    parts = len(fresh_keys)
    sources = cached.shape[0]
    keys_count = bias.shape[1]
    rows = keys_count // sources
    tile = 128
    contract = (((1,), (1,)), ((), ()))

    def body(*refs):
        q_ref, c_ref, b_ref = refs[:3]
        key_refs = refs[3 : 3 + parts]
        value_refs = refs[3 + parts : 3 + 2 * parts]
        o_ref, old_values, new_values = refs[-3:]
        old_values[:, :HD] = c_ref[:, rows:].reshape(keys_count, HD)
        old_values[:, HD:] = jnp.ones((keys_count, HD), BF16)
        for i in range(parts):
            new_values[i * tokens : (i + 1) * tokens, :HD] = value_refs[i][0]
        new_values[:, HD:] = jnp.ones((tokens * parts, HD), BF16)
        cached_keys = c_ref[:, :rows].reshape(keys_count, HD)

        def product(q, keys):
            return lax.dot_general(q, keys, contract, preferred_element_type=F32)

        def scores(g, t):
            q = q_ref[g, t * tile : (t + 1) * tile]
            width = (t + 1) * tile
            out = [product(q, cached_keys) + b_ref[...]]
            out += [product(q, ref[0]) for ref in key_refs[:-1]]
            row = lax.broadcasted_iota(jnp.int32, (tile, width), 0) + t * tile
            col = lax.broadcasted_iota(jnp.int32, (tile, width), 1)
            out.append(jnp.where(col <= row, product(q, key_refs[-1][0, :width]), masked_score))
            return out

        work = [(g, t) for g in range(group) for t in range(tokens // tile)]
        ahead = scores(*work[0])
        for i, (g, t) in enumerate(work):
            now = ahead
            if i + 1 < len(work):
                ahead = scores(*work[i + 1])
            top = jnp.max(now[0], axis=1, keepdims=True)
            for part in now[1:]:
                top = jnp.maximum(top, jnp.max(part, axis=1, keepdims=True))
            now = [jnp.exp2(part - top).astype(BF16) for part in now]
            mixed = jnp.dot(now[0], old_values[...], preferred_element_type=F32)
            start = 0
            for part in now[1:]:
                values = new_values[start : start + part.shape[1]]
                mixed = mixed + jnp.dot(part, values, preferred_element_type=F32)
                start += part.shape[1]
            o_ref[t * tile : (t + 1) * tile, g * HD : (g + 1) * HD] = (
                mixed[:, :HD] / mixed[:, HD:]
            ).astype(BF16)

    head_spec = pl.BlockSpec((1, tokens, HD), lambda h: (first + h, 0, 0))
    in_specs = [
        pl.BlockSpec((group, tokens, HD), lambda h: (first + h, 0, 0)),
        pl.BlockSpec((sources, 2 * rows, HD), lambda h: (0, at + h, 0)),
        pl.BlockSpec((1, keys_count), lambda h: (0, 0)),
    ] + [head_spec] * (2 * parts)
    operands = [queries, cached, bias] + list(fresh_keys) + list(fresh_values)
    aliases = {}
    if attended is not None:
        aliases = {len(operands): 0}
        in_specs.append(pl.BlockSpec(memory_space=pl.ANY))
        operands.append(attended)
    pairs = count * group * tokens * (keys_count + tokens * parts)
    return pl.pallas_call(
        body,
        grid=(count,),
        in_specs=in_specs,
        out_specs=pl.BlockSpec((tokens, group * HD), lambda h: (0, first + h)),
        out_shape=jax.ShapeDtypeStruct((tokens, heads * HD), BF16),
        scratch_shapes=[
            pltpu.VMEM((keys_count, 2 * HD), BF16),
            pltpu.VMEM((tokens * parts, 2 * HD), BF16),
        ],
        input_output_aliases=aliases,
        compiler_params=params(1),
        cost_estimate=cost(8 * pairs * HD, 4 * count * keys_count * HD, pairs),
        name="attend",
    )(*operands)


def project_out(col_block, attended, weight, width, strips, kind, depth, at=0, add=None):
    rows = attended.shape[0]
    strip = rows // strips
    step = min(1024, width)
    steps = width // step

    def body(cols, x_ref, w_ref, *refs):
        total = jnp.dot(x_ref[...], w_ref[...], preferred_element_type=F32)
        if add is not None:
            total = total + refs[0][...]
        for i in range(strips):
            refs[i - strips][...] = total[i * strip : (i + 1) * strip].astype(kind)

    in_specs = [
        pl.BlockSpec((rows, depth), lambda n, cols: (0, at)),
        pl.BlockSpec((depth, step), lambda n, cols: (at, cols[0] * steps + n)),
    ]
    operands = [attended, weight]
    if add is not None:
        in_specs.append(pl.BlockSpec((rows, step), lambda n, cols: (0, n)))
        operands.append(add)
    return pl.pallas_call(
        body,
        grid_spec=pltpu.PrefetchScalarGridSpec(
            num_scalar_prefetch=1,
            grid=(steps,),
            in_specs=in_specs,
            out_specs=[pl.BlockSpec((strip, step), lambda n, cols: (0, n))] * strips,
        ),
        out_shape=[jax.ShapeDtypeStruct((strip, width), kind)] * strips,
        compiler_params=params(1),
        cost_estimate=cost(2 * rows * depth * width, depth * width * 2 + rows * width * 4),
        name="project_out",
    )(col_block, *operands)


def combine(own, parts, index, total_rows, out):
    rows, width = own.shape

    def body(*refs):
        total = refs[0][...]
        for ref in refs[1 : 1 + len(parts)]:
            total = total + ref[...].astype(F32)
        refs[-1][...] = total.astype(BF16)

    step = min(1024, width)
    in_specs = [pl.BlockSpec((rows, step), lambda n: (0, n))] * (1 + len(parts))
    operands = [own] + list(parts)
    aliases = {}
    if out is not None:
        aliases = {len(operands): 0}
        in_specs.append(pl.BlockSpec(memory_space=pl.ANY))
        operands.append(out)
    return pl.pallas_call(
        body,
        grid=(width // step,),
        in_specs=in_specs,
        out_specs=pl.BlockSpec((rows, step), lambda n: (index, n)),
        out_shape=jax.ShapeDtypeStruct((total_rows, width), BF16),
        input_output_aliases=aliases,
        compiler_params=params(1),
        cost_estimate=cost(0, rows * width * 8),
        name="combine",
    )(*operands)


def rotation(length, tokens):
    half = HD // 2
    freqs = jnp.exp(jnp.arange(half, dtype=F32) * (-2.0 * math.log(ROPE_BASE) / HD))
    positions = (length + jnp.arange(tokens, dtype=jnp.int32)).astype(F32)
    angles = positions[:, None] * freqs[None, :]
    cosine = jnp.cos(angles)
    sine = jnp.sin(angles)
    return jnp.concatenate([cosine, cosine], axis=1), jnp.concatenate([-sine, sine], axis=1)


def on_device(
    hidden, w_query, w_key, w_value, w_out, cache_keys, cache_values, cached_len, page_table
):
    tokens = hidden.shape[0]
    assert tokens == NEW
    seq = lax.axis_size("seq")
    tp = lax.axis_size("tp")
    query_heads = w_query.shape[1] // HD
    kv_heads = w_key.shape[1] // HD
    group = query_heads // kv_heads
    block_len = cache_keys.shape[1]
    per_peer = max(1, CTX // block_len // seq)
    request = lax.axis_index("seq")
    rank = lax.axis_index("tp")
    length = cached_len[request]

    span = per_peer * block_len
    split = [(0, kv_heads - 1), (kv_heads - 1, 1)] if kv_heads > 1 else [(0, 1)]
    own_row = jnp.reshape(rank, (1,)).astype(jnp.int32)
    rest_rows = jnp.stack([(rank - shift) % tp for shift in range(1, tp)]).astype(jnp.int32)
    cosine, sine = rotation(length, tokens)

    def pick(first, count):
        return pick_blocks(
            page_table, cached_len, cache_keys, cache_values, first, count, seq, per_peer
        )

    def exchange(block):
        return lax.all_to_all(block, "seq", 0, 0, tiled=True)

    def swap(x, shift):
        return lax.ppermute(x, "tp", [(i, (i + shift) % tp) for i in range(tp)])

    half_tokens = tokens // 2
    received = [exchange(pick(*split[0]))]
    arrivals = []
    for half in range(2):
        mine = hidden[half * half_tokens : (half + 1) * half_tokens]
        if arrivals:
            mine, arrivals[0][0] = lax.optimization_barrier((mine, arrivals[0][0]))
        arrivals.append([swap(mine, shift) for shift in range(1, tp)])
    own_parts = [project_own(own_row, hidden, w) for w in (w_key, w_value, w_query)]

    def rest(half, parts):
        def one(weight, part, scale):
            return project_rest(
                rest_rows, half, arrivals[half], weight, part, cosine, sine, scale
            )

        return [
            one(w_key, parts[0], 1.0),
            one(w_value, parts[1], None),
            one(w_query, parts[2], HD ** (-0.5) / math.log(2.0)),
        ]

    fresh = [rest(0, own_parts), rest(1, own_parts)]
    for first, count in split[1:]:
        block, received[-1], fresh = lax.optimization_barrier(
            (pick(first, count), received[-1], fresh)
        )
        received.append(exchange(block))
    bias = received[0][:, 2 * span * split[0][1], :span].astype(F32).reshape(1, seq * span)
    attended = [None, None]

    def run(first, count, half):
        piece = 0 if first < split[0][1] else 1
        attended[half] = attend(
            first,
            count,
            first - split[piece][0],
            group,
            fresh[half][2],
            [fresh[i][0] for i in range(half + 1)],
            [fresh[i][1] for i in range(half + 1)],
            received[piece],
            bias,
            attended[half],
        )

    width = w_out.shape[1] // tp
    targets = [jnp.reshape((rank + s) % tp, (1,)).astype(jnp.int32) for s in range(1, tp)]
    features = query_heads * HD
    per_head = group * HD
    early = per_head * split[0][1] if len(split) > 1 else features

    run(*split[0], 0)
    sums = []
    if len(split) > 1:
        sums = [project_out(t, attended[0], w_out, width, 1, F32, early)[0] for t in targets]
        received[1], attended, sums = lax.optimization_barrier(
            (received[1], attended, sums)
        )
        run(*split[1], 0)
        late = features - early
        other = [
            project_out(t, attended[0], w_out, width, 1, BF16, late, early // late, part)
            for t, part in zip(targets, sums)
        ]
    else:
        other = [project_out(t, attended[0], w_out, width, 1, BF16, features) for t in targets]
    other = [[swap(part[0], shift + 1)] for shift, part in enumerate(other)]
    run(*split[0], 1)
    if len(split) > 1:
        run(*split[1], 1)
    strips = 2 if tp == 2 else 1
    for shift, target in enumerate(targets):
        parts = project_out(target, attended[1], w_out, width, strips, BF16, features)
        if shift == 0 and tp == 2:
            parts, other[0] = lax.optimization_barrier((parts, other[0]))
        other[shift] += [swap(part, shift + 1) for part in parts]
    own = project_out(own_row, attended[0], w_out, width, 1, F32, features)
    own += project_out(own_row, attended[1], w_out, width, strips, F32, features)
    out = None
    row = 0
    for i, part in enumerate(own):
        out = combine(part, [arrived[i] for arrived in other], row // part.shape[0], tokens, out)
        row += part.shape[0]
    return out


def solution(mesh):
    in_specs = (
        P("seq", "tp"),
        P(None, "tp"),
        P(None, "tp"),
        P(None, "tp"),
        P("tp", None),
        P("seq", None, "tp"),
        P("seq", None, "tp"),
        P(),
        P("seq", None),
    )
    out_specs = P("seq", "tp")
    return jax.shard_map(
        on_device, mesh=mesh, in_specs=in_specs, out_specs=out_specs, check_vma=False
    )
```

```python
import math

import jax
import jax.numpy as jnp
from jax import lax
from jax.experimental import pallas as pl
from jax.experimental.pallas import tpu as pltpu
from jax.sharding import PartitionSpec as P

HD = 128
NEW = 512
CTX = 2048
ROPE_BASE = 1000000.0
masked_score = -1e30
VMEM_LIMIT = 56 * 1024 * 1024
BF16 = jnp.bfloat16
F32 = jnp.float32


def params(count):
    return pltpu.CompilerParams(
        dimension_semantics=("arbitrary",) * count, vmem_limit_bytes=VMEM_LIMIT
    )


def cost(flops, moved, exps=0):
    return pl.CostEstimate(flops=flops, bytes_accessed=moved, transcendentals=exps)


def pick_blocks(page_table, cached_len, cache_keys, cache_values, first, count, seq, per_peer):
    masked = first == 0
    blocks, block_len, _ = cache_keys.shape
    span = per_peer * block_len
    rows = 2 * span * count + (8 if masked else 0)
    width = count * HD

    def body(table, lengths, keys, values, out, index):
        for slot in range(seq * per_peer):
            index[slot] = 0
        tally = seq * per_peer
        for r in range(seq):
            index[tally + r] = 0

        def place(b, carry):
            r = table[b, 0]
            taken = index[tally + r]
            index[r * per_peer + jnp.minimum(taken, per_peer - 1)] = b
            index[tally + r] = taken + 1
            return carry

        lax.fori_loop(0, blocks, place, 0)
        lane = lax.broadcasted_iota(jnp.int32, (8, HD), 1)
        for r in range(seq):
            mask = jnp.full((8, HD), masked_score, F32)
            for k in range(per_peer):
                b = index[r * per_peer + k]
                for h in range(count):
                    at = 2 * h * span + k * block_len
                    columns = slice(h * HD, (h + 1) * HD)
                    out[r, at : at + block_len, :] = keys[b, :, columns]
                    out[r, at + span : at + span + block_len, :] = values[b, :, columns]
                if masked:
                    filled = jnp.minimum(lengths[r] - table[b, 1] * block_len, block_len)
                    filled = jnp.where(index[tally + r] > k, filled, 0)
                    inside = (lane >= k * block_len) & (lane < k * block_len + filled)
                    mask = jnp.where(inside, 0.0, mask)
            if masked:
                out[r, 2 * span * count :, :] = mask.astype(BF16)

    part = pl.BlockSpec((blocks, block_len, width), lambda i: (0, 0, first // count))
    return pl.pallas_call(
        body,
        grid=(1,),
        in_specs=[
            pl.BlockSpec(memory_space=pltpu.SMEM),
            pl.BlockSpec(memory_space=pltpu.SMEM),
            part,
            part,
        ],
        out_specs=pl.BlockSpec((seq, rows, HD), lambda i: (0, 0, 0)),
        out_shape=jax.ShapeDtypeStruct((seq, rows, HD), BF16),
        scratch_shapes=[pltpu.SMEM((seq * per_peer + seq,), jnp.int32)],
        compiler_params=params(1),
        cost_estimate=cost(0, 2 * seq * rows * HD * 2),
        name="pick_blocks",
    )(page_table, cached_len, cache_keys, cache_values)


def project_own(row_block, x, weight):
    tokens, depth = x.shape
    width = weight.shape[1]
    step = min(512, width)

    def body(rows, x_ref, w_ref, o_ref):
        o_ref[...] = jnp.dot(x_ref[...], w_ref[...], preferred_element_type=F32)

    return pl.pallas_call(
        body,
        grid_spec=pltpu.PrefetchScalarGridSpec(
            num_scalar_prefetch=1,
            grid=(width // step,),
            in_specs=[
                pl.BlockSpec((tokens, depth), lambda n, rows: (0, 0)),
                pl.BlockSpec((depth, step), lambda n, rows: (rows[0], n)),
            ],
            out_specs=pl.BlockSpec((tokens, step), lambda n, rows: (0, n)),
        ),
        out_shape=jax.ShapeDtypeStruct((tokens, width), F32),
        compiler_params=params(1),
        cost_estimate=cost(2 * tokens * depth * width, depth * width * 2 + tokens * width * 4),
        name="project_own",
    )(row_block, x, weight)


def project_rest(row_blocks, half, pieces, weight, partial, cosine, sine, scale):
    tokens, depth = pieces[0].shape
    count = len(pieces)
    width = weight.shape[1]
    step = min(512, width)
    heads = step // HD

    def body(rows, *refs):
        x_refs = refs[:count]
        w_refs = refs[count : 2 * count]
        p_ref, c_ref, s_ref, o_ref = refs[2 * count :]
        total = p_ref[...]
        for x_ref, w_ref in zip(x_refs, w_refs):
            total = total + jnp.dot(x_ref[...], w_ref[...], preferred_element_type=F32)
        for h in range(heads):
            u = total[:, h * HD : (h + 1) * HD]
            if scale is not None:
                inverse = lax.rsqrt(jnp.mean(u * u, axis=-1, keepdims=True) + 1e-06) * scale
                u = u * inverse
                u = u * c_ref[...] + pltpu.roll(u, HD // 2, 1) * s_ref[...]
            o_ref[h] = u.astype(BF16)

    def weight_spec(i):
        return pl.BlockSpec((depth, step), lambda n, rows: (rows[i], n))

    return pl.pallas_call(
        body,
        grid_spec=pltpu.PrefetchScalarGridSpec(
            num_scalar_prefetch=1,
            grid=(width // step,),
            in_specs=[pl.BlockSpec((tokens, depth), lambda n, rows: (0, 0))] * count
            + [weight_spec(i) for i in range(count)]
            + [
                pl.BlockSpec((tokens, step), lambda n, rows: (half, n)),
                pl.BlockSpec((tokens, HD), lambda n, rows: (half, 0)),
                pl.BlockSpec((tokens, HD), lambda n, rows: (half, 0)),
            ],
            out_specs=pl.BlockSpec((heads, tokens, HD), lambda n, rows: (n, 0, 0)),
        ),
        out_shape=jax.ShapeDtypeStruct((width // HD, tokens, HD), BF16),
        compiler_params=params(1),
        cost_estimate=cost(
            2 * tokens * depth * count * width, depth * count * width * 2 + tokens * width * 8
        ),
        name="project_rest",
    )(row_blocks, *pieces, *([weight] * count), partial, cosine, sine)


def attend(first, count, at, group, queries, fresh_keys, fresh_values, cached, bias, attended):
    heads, tokens, _ = queries.shape
    parts = len(fresh_keys)
    sources = cached.shape[0]
    keys_count = bias.shape[1]
    rows = keys_count // sources
    tile = 128
    contract = (((1,), (1,)), ((), ()))

    def body(*refs):
        q_ref, c_ref, b_ref = refs[:3]
        key_refs = refs[3 : 3 + parts]
        value_refs = refs[3 + parts : 3 + 2 * parts]
        o_ref, old_values, new_values = refs[-3:]
        old_values[:, :HD] = c_ref[:, rows:].reshape(keys_count, HD)
        old_values[:, HD:] = jnp.ones((keys_count, HD), BF16)
        for i in range(parts):
            new_values[i * tokens : (i + 1) * tokens, :HD] = value_refs[i][0]
        new_values[:, HD:] = jnp.ones((tokens * parts, HD), BF16)
        cached_keys = c_ref[:, :rows].reshape(keys_count, HD)

        def product(q, keys):
            return lax.dot_general(q, keys, contract, preferred_element_type=F32)

        def scores(g, t):
            q = q_ref[g, t * tile : (t + 1) * tile]
            width = (t + 1) * tile
            out = [product(q, cached_keys) + b_ref[...]]
            out += [product(q, ref[0]) for ref in key_refs[:-1]]
            row = lax.broadcasted_iota(jnp.int32, (tile, width), 0) + t * tile
            col = lax.broadcasted_iota(jnp.int32, (tile, width), 1)
            out.append(jnp.where(col <= row, product(q, key_refs[-1][0, :width]), masked_score))
            return out

        work = [(g, t) for g in range(group) for t in range(tokens // tile)]
        ahead = scores(*work[0])
        for i, (g, t) in enumerate(work):
            now = ahead
            if i + 1 < len(work):
                ahead = scores(*work[i + 1])
            top = jnp.max(now[0], axis=1, keepdims=True)
            for part in now[1:]:
                top = jnp.maximum(top, jnp.max(part, axis=1, keepdims=True))
            now = [jnp.exp2(part - top).astype(BF16) for part in now]
            mixed = jnp.dot(now[0], old_values[...], preferred_element_type=F32)
            start = 0
            for part in now[1:]:
                values = new_values[start : start + part.shape[1]]
                mixed = mixed + jnp.dot(part, values, preferred_element_type=F32)
                start += part.shape[1]
            o_ref[t * tile : (t + 1) * tile, g * HD : (g + 1) * HD] = (
                mixed[:, :HD] / mixed[:, HD:]
            ).astype(BF16)

    head_spec = pl.BlockSpec((1, tokens, HD), lambda h: (first + h, 0, 0))
    in_specs = [
        pl.BlockSpec((group, tokens, HD), lambda h: (first + h, 0, 0)),
        pl.BlockSpec((sources, 2 * rows, HD), lambda h: (0, at + h, 0)),
        pl.BlockSpec((1, keys_count), lambda h: (0, 0)),
    ] + [head_spec] * (2 * parts)
    operands = [queries, cached, bias] + list(fresh_keys) + list(fresh_values)
    aliases = {}
    if attended is not None:
        aliases = {len(operands): 0}
        in_specs.append(pl.BlockSpec(memory_space=pl.ANY))
        operands.append(attended)
    pairs = count * group * tokens * (keys_count + tokens * parts)
    return pl.pallas_call(
        body,
        grid=(count,),
        in_specs=in_specs,
        out_specs=pl.BlockSpec((tokens, group * HD), lambda h: (0, first + h)),
        out_shape=jax.ShapeDtypeStruct((tokens, heads * HD), BF16),
        scratch_shapes=[
            pltpu.VMEM((keys_count, 2 * HD), BF16),
            pltpu.VMEM((tokens * parts, 2 * HD), BF16),
        ],
        input_output_aliases=aliases,
        compiler_params=params(1),
        cost_estimate=cost(8 * pairs * HD, 4 * count * keys_count * HD, pairs),
        name="attend",
    )(*operands)


def project_out(col_block, attended, weight, width, strips, kind, depth, at=0, add=None):
    rows = attended.shape[0]
    strip = rows // strips
    step = min(1024, width)
    steps = width // step

    def body(cols, x_ref, w_ref, *refs):
        total = jnp.dot(x_ref[...], w_ref[...], preferred_element_type=F32)
        if add is not None:
            total = total + refs[0][...]
        for i in range(strips):
            refs[i - strips][...] = total[i * strip : (i + 1) * strip].astype(kind)

    in_specs = [
        pl.BlockSpec((rows, depth), lambda n, cols: (0, at)),
        pl.BlockSpec((depth, step), lambda n, cols: (at, cols[0] * steps + n)),
    ]
    operands = [attended, weight]
    if add is not None:
        in_specs.append(pl.BlockSpec((rows, step), lambda n, cols: (0, n)))
        operands.append(add)
    return pl.pallas_call(
        body,
        grid_spec=pltpu.PrefetchScalarGridSpec(
            num_scalar_prefetch=1,
            grid=(steps,),
            in_specs=in_specs,
            out_specs=[pl.BlockSpec((strip, step), lambda n, cols: (0, n))] * strips,
        ),
        out_shape=[jax.ShapeDtypeStruct((strip, width), kind)] * strips,
        compiler_params=params(1),
        cost_estimate=cost(2 * rows * depth * width, depth * width * 2 + rows * width * 4),
        name="project_out",
    )(col_block, *operands)


def combine(own, parts, index, total_rows, out):
    rows, width = own.shape

    def body(*refs):
        total = refs[0][...]
        for ref in refs[1 : 1 + len(parts)]:
            total = total + ref[...].astype(F32)
        refs[-1][...] = total.astype(BF16)

    step = width
    in_specs = [pl.BlockSpec((rows, step), lambda n: (0, n))] * (1 + len(parts))
    operands = [own] + list(parts)
    aliases = {}
    if out is not None:
        aliases = {len(operands): 0}
        in_specs.append(pl.BlockSpec(memory_space=pl.ANY))
        operands.append(out)
    return pl.pallas_call(
        body,
        grid=(width // step,),
        in_specs=in_specs,
        out_specs=pl.BlockSpec((rows, step), lambda n: (index, n)),
        out_shape=jax.ShapeDtypeStruct((total_rows, width), BF16),
        input_output_aliases=aliases,
        compiler_params=params(1),
        cost_estimate=cost(0, rows * width * 8),
        name="combine",
    )(*operands)


def rotation(length, tokens):
    half = HD // 2
    freqs = jnp.exp(jnp.arange(half, dtype=F32) * (-2.0 * math.log(ROPE_BASE) / HD))
    positions = (length + jnp.arange(tokens, dtype=jnp.int32)).astype(F32)
    angles = positions[:, None] * freqs[None, :]
    cosine = jnp.cos(angles)
    sine = jnp.sin(angles)
    return jnp.concatenate([cosine, cosine], axis=1), jnp.concatenate([-sine, sine], axis=1)


def on_device(
    hidden, w_query, w_key, w_value, w_out, cache_keys, cache_values, cached_len, page_table
):
    tokens = hidden.shape[0]
    assert tokens == NEW
    seq = lax.axis_size("seq")
    tp = lax.axis_size("tp")
    query_heads = w_query.shape[1] // HD
    kv_heads = w_key.shape[1] // HD
    group = query_heads // kv_heads
    block_len = cache_keys.shape[1]
    per_peer = max(1, CTX // block_len // seq)
    request = lax.axis_index("seq")
    rank = lax.axis_index("tp")
    length = cached_len[request]

    span = per_peer * block_len
    split = [(0, kv_heads - 1), (kv_heads - 1, 1)] if kv_heads > 1 else [(0, 1)]
    own_row = jnp.reshape(rank, (1,)).astype(jnp.int32)
    rest_rows = jnp.stack([(rank - shift) % tp for shift in range(1, tp)]).astype(jnp.int32)
    cosine, sine = rotation(length, tokens)

    def pick(first, count):
        return pick_blocks(
            page_table, cached_len, cache_keys, cache_values, first, count, seq, per_peer
        )

    def exchange(block):
        return lax.all_to_all(block, "seq", 0, 0, tiled=True)

    def swap(x, shift):
        return lax.ppermute(x, "tp", [(i, (i + shift) % tp) for i in range(tp)])

    half_tokens = tokens // 2
    received = [exchange(pick(*split[0]))]
    arrivals = []
    for half in range(2):
        mine = hidden[half * half_tokens : (half + 1) * half_tokens]
        if arrivals:
            mine, arrivals[0][0] = lax.optimization_barrier((mine, arrivals[0][0]))
        arrivals.append([swap(mine, shift) for shift in range(1, tp)])
    own_parts = [project_own(own_row, hidden, w) for w in (w_key, w_value, w_query)]

    def rest(half, parts):
        def one(weight, part, scale):
            return project_rest(
                rest_rows, half, arrivals[half], weight, part, cosine, sine, scale
            )

        return [
            one(w_key, parts[0], 1.0),
            one(w_value, parts[1], None),
            one(w_query, parts[2], HD ** (-0.5) / math.log(2.0)),
        ]

    fresh = [rest(0, own_parts), rest(1, own_parts)]
    for first, count in split[1:]:
        block, received[-1], fresh = lax.optimization_barrier(
            (pick(first, count), received[-1], fresh)
        )
        received.append(exchange(block))
    bias = received[0][:, 2 * span * split[0][1], :span].astype(F32).reshape(1, seq * span)
    attended = [None, None]

    def run(first, count, half):
        piece = 0 if first < split[0][1] else 1
        attended[half] = attend(
            first,
            count,
            first - split[piece][0],
            group,
            fresh[half][2],
            [fresh[i][0] for i in range(half + 1)],
            [fresh[i][1] for i in range(half + 1)],
            received[piece],
            bias,
            attended[half],
        )

    width = w_out.shape[1] // tp
    targets = [jnp.reshape((rank + s) % tp, (1,)).astype(jnp.int32) for s in range(1, tp)]
    features = query_heads * HD
    per_head = group * HD
    early = per_head * split[0][1] if len(split) > 1 else features

    run(*split[0], 0)
    sums = []
    if len(split) > 1:
        sums = [project_out(t, attended[0], w_out, width, 1, F32, early)[0] for t in targets]
        received[1], attended, sums = lax.optimization_barrier(
            (received[1], attended, sums)
        )
        run(*split[1], 0)
        late = features - early
        other = [
            project_out(t, attended[0], w_out, width, 1, BF16, late, early // late, part)
            for t, part in zip(targets, sums)
        ]
    else:
        other = [project_out(t, attended[0], w_out, width, 1, BF16, features) for t in targets]
    other = [[swap(part[0], shift + 1)] for shift, part in enumerate(other)]
    run(*split[0], 1)
    if len(split) > 1:
        run(*split[1], 1)
    strips = 2 if tp == 2 else 1
    for shift, target in enumerate(targets):
        parts = project_out(target, attended[1], w_out, width, strips, BF16, features)
        other[shift] += [swap(part, shift + 1) for part in parts]
    if tp == 2:
        other[0][0], attended = lax.optimization_barrier((other[0][0], attended))
    own = project_out(own_row, attended[0], w_out, width, 1, F32, features)
    own += project_out(own_row, attended[1], w_out, width, strips, F32, features)
    out = None
    row = 0
    for i, part in enumerate(own):
        if i == len(own) - 1:
            total = part
            for arrived in other:
                total = total + arrived[i].astype(F32)
            return lax.dynamic_update_slice(out, total.astype(BF16), (row, 0))
        out = combine(part, [arrived[i] for arrived in other], row // part.shape[0], tokens, out)
        row += part.shape[0]
    return out


def solution(mesh):
    in_specs = (
        P("seq", "tp"),
        P(None, "tp"),
        P(None, "tp"),
        P(None, "tp"),
        P("tp", None),
        P("seq", None, "tp"),
        P("seq", None, "tp"),
        P(),
        P("seq", None),
    )
    out_specs = P("seq", "tp")
    return jax.shard_map(
        on_device, mesh=mesh, in_specs=in_specs, out_specs=out_specs, check_vma=False
    )
```

```python
import math

import jax
import jax.numpy as jnp
from jax import lax
from jax.experimental import pallas as pl
from jax.experimental.pallas import tpu as pltpu
from jax.sharding import PartitionSpec as P

HD = 128
NEW = 512
CTX = 2048
ROPE_BASE = 1000000.0
masked_score = -1e30
VMEM_LIMIT = 40 * 1024 * 1024
BF16 = jnp.bfloat16
F32 = jnp.float32


def params(count):
    return pltpu.CompilerParams(
        dimension_semantics=("arbitrary",) * count, vmem_limit_bytes=VMEM_LIMIT
    )


def cost(flops, moved, exps=0):
    return pl.CostEstimate(flops=flops, bytes_accessed=moved, transcendentals=exps)


def pick_blocks(page_table, cached_len, cache_keys, cache_values, first, count, seq, per_peer):
    masked = first == 0
    blocks, block_len, _ = cache_keys.shape
    span = per_peer * block_len
    rows = 2 * span * count + (8 if masked else 0)
    width = count * HD

    def body(table, lengths, keys, values, out, index):
        for slot in range(seq * per_peer):
            index[slot] = 0
        tally = seq * per_peer
        for r in range(seq):
            index[tally + r] = 0

        def place(b, carry):
            r = table[b, 0]
            taken = index[tally + r]
            index[r * per_peer + jnp.minimum(taken, per_peer - 1)] = b
            index[tally + r] = taken + 1
            return carry

        lax.fori_loop(0, blocks, place, 0)
        lane = lax.broadcasted_iota(jnp.int32, (8, HD), 1)
        for r in range(seq):
            mask = jnp.full((8, HD), masked_score, F32)
            for k in range(per_peer):
                b = index[r * per_peer + k]
                for h in range(count):
                    at = 2 * h * span + k * block_len
                    columns = slice(h * HD, (h + 1) * HD)
                    out[r, at : at + block_len, :] = keys[b, :, columns]
                    out[r, at + span : at + span + block_len, :] = values[b, :, columns]
                if masked:
                    filled = jnp.minimum(lengths[r] - table[b, 1] * block_len, block_len)
                    filled = jnp.where(index[tally + r] > k, filled, 0)
                    inside = (lane >= k * block_len) & (lane < k * block_len + filled)
                    mask = jnp.where(inside, 0.0, mask)
            if masked:
                out[r, 2 * span * count :, :] = mask.astype(BF16)

    part = pl.BlockSpec((blocks, block_len, width), lambda i: (0, 0, first // count))
    return pl.pallas_call(
        body,
        grid=(1,),
        in_specs=[
            pl.BlockSpec(memory_space=pltpu.SMEM),
            pl.BlockSpec(memory_space=pltpu.SMEM),
            part,
            part,
        ],
        out_specs=pl.BlockSpec((seq, rows, HD), lambda i: (0, 0, 0)),
        out_shape=jax.ShapeDtypeStruct((seq, rows, HD), BF16),
        scratch_shapes=[pltpu.SMEM((seq * per_peer + seq,), jnp.int32)],
        compiler_params=params(1),
        cost_estimate=cost(0, 2 * seq * rows * HD * 2),
        name="pick_blocks",
    )(page_table, cached_len, cache_keys, cache_values)


def project_own(row_block, x, weight):
    tokens, depth = x.shape
    width = weight.shape[1]
    step = min(512, width)

    def body(rows, x_ref, w_ref, o_ref):
        o_ref[...] = jnp.dot(x_ref[...], w_ref[...], preferred_element_type=F32)

    return pl.pallas_call(
        body,
        grid_spec=pltpu.PrefetchScalarGridSpec(
            num_scalar_prefetch=1,
            grid=(width // step,),
            in_specs=[
                pl.BlockSpec((tokens, depth), lambda n, rows: (0, 0)),
                pl.BlockSpec((depth, step), lambda n, rows: (rows[0], n)),
            ],
            out_specs=pl.BlockSpec((tokens, step), lambda n, rows: (0, n)),
        ),
        out_shape=jax.ShapeDtypeStruct((tokens, width), F32),
        compiler_params=params(1),
        cost_estimate=cost(2 * tokens * depth * width, depth * width * 2 + tokens * width * 4),
        name="project_own",
    )(row_block, x, weight)


def project_rest(row_blocks, half, pieces, weight, partial, cosine, sine, scale):
    tokens, depth = pieces[0].shape
    count = len(pieces)
    width = weight.shape[1]
    step = min(512, width)
    heads = step // HD

    def body(rows, *refs):
        x_refs = refs[:count]
        w_refs = refs[count : 2 * count]
        p_ref, c_ref, s_ref, o_ref = refs[2 * count :]
        total = p_ref[...]
        for x_ref, w_ref in zip(x_refs, w_refs):
            total = total + jnp.dot(x_ref[...], w_ref[...], preferred_element_type=F32)
        for h in range(heads):
            u = total[:, h * HD : (h + 1) * HD]
            if scale is not None:
                inverse = lax.rsqrt(jnp.mean(u * u, axis=-1, keepdims=True) + 1e-06) * scale
                u = u * inverse
                u = u * c_ref[...] + pltpu.roll(u, HD // 2, 1) * s_ref[...]
            o_ref[h] = u.astype(BF16)

    def weight_spec(i):
        return pl.BlockSpec((depth, step), lambda n, rows: (rows[i], n))

    return pl.pallas_call(
        body,
        grid_spec=pltpu.PrefetchScalarGridSpec(
            num_scalar_prefetch=1,
            grid=(width // step,),
            in_specs=[pl.BlockSpec((tokens, depth), lambda n, rows: (0, 0))] * count
            + [weight_spec(i) for i in range(count)]
            + [
                pl.BlockSpec((tokens, step), lambda n, rows: (half, n)),
                pl.BlockSpec((tokens, HD), lambda n, rows: (half, 0)),
                pl.BlockSpec((tokens, HD), lambda n, rows: (half, 0)),
            ],
            out_specs=pl.BlockSpec((heads, tokens, HD), lambda n, rows: (n, 0, 0)),
        ),
        out_shape=jax.ShapeDtypeStruct((width // HD, tokens, HD), BF16),
        compiler_params=params(1),
        cost_estimate=cost(
            2 * tokens * depth * count * width, depth * count * width * 2 + tokens * width * 8
        ),
        name="project_rest",
    )(row_blocks, *pieces, *([weight] * count), partial, cosine, sine)


def attend(first, count, at, group, queries, fresh_keys, fresh_values, cached, bias, attended):
    heads, tokens, _ = queries.shape
    parts = len(fresh_keys)
    sources = cached.shape[0]
    keys_count = bias.shape[1]
    rows = keys_count // sources
    tile = 128
    contract = (((1,), (1,)), ((), ()))

    def body(*refs):
        q_ref, c_ref, b_ref = refs[:3]
        key_refs = refs[3 : 3 + parts]
        value_refs = refs[3 + parts : 3 + 2 * parts]
        o_ref, old_values, new_values = refs[-3:]
        old_values[:, :HD] = c_ref[:, rows:].reshape(keys_count, HD)
        old_values[:, HD:] = jnp.ones((keys_count, HD), BF16)
        for i in range(parts):
            new_values[i * tokens : (i + 1) * tokens, :HD] = value_refs[i][0]
        new_values[:, HD:] = jnp.ones((tokens * parts, HD), BF16)
        cached_keys = c_ref[:, :rows].reshape(keys_count, HD)

        def product(q, keys):
            return lax.dot_general(q, keys, contract, preferred_element_type=F32)

        def scores(g, t):
            q = q_ref[g, t * tile : (t + 1) * tile]
            width = (t + 1) * tile
            out = [product(q, cached_keys) + b_ref[...]]
            out += [product(q, ref[0]) for ref in key_refs[:-1]]
            row = lax.broadcasted_iota(jnp.int32, (tile, width), 0) + t * tile
            col = lax.broadcasted_iota(jnp.int32, (tile, width), 1)
            out.append(jnp.where(col <= row, product(q, key_refs[-1][0, :width]), masked_score))
            return out

        work = [(g, t) for g in range(group) for t in range(tokens // tile)]
        ahead = scores(*work[0])
        for i, (g, t) in enumerate(work):
            now = ahead
            if i + 1 < len(work):
                ahead = scores(*work[i + 1])
            top = jnp.max(now[0], axis=1, keepdims=True)
            for part in now[1:]:
                top = jnp.maximum(top, jnp.max(part, axis=1, keepdims=True))
            now = [jnp.exp2(part - top).astype(BF16) for part in now]
            mixed = jnp.dot(now[0], old_values[...], preferred_element_type=F32)
            start = 0
            for part in now[1:]:
                values = new_values[start : start + part.shape[1]]
                mixed = mixed + jnp.dot(part, values, preferred_element_type=F32)
                start += part.shape[1]
            o_ref[t * tile : (t + 1) * tile, g * HD : (g + 1) * HD] = (
                mixed[:, :HD] / mixed[:, HD:]
            ).astype(BF16)

    head_spec = pl.BlockSpec((1, tokens, HD), lambda h: (first + h, 0, 0))
    in_specs = [
        pl.BlockSpec((group, tokens, HD), lambda h: (first + h, 0, 0)),
        pl.BlockSpec((sources, 2 * rows, HD), lambda h: (0, at + h, 0)),
        pl.BlockSpec((1, keys_count), lambda h: (0, 0)),
    ] + [head_spec] * (2 * parts)
    operands = [queries, cached, bias] + list(fresh_keys) + list(fresh_values)
    aliases = {}
    if attended is not None:
        aliases = {len(operands): 0}
        in_specs.append(pl.BlockSpec(memory_space=pl.ANY))
        operands.append(attended)
    pairs = count * group * tokens * (keys_count + tokens * parts)
    return pl.pallas_call(
        body,
        grid=(count,),
        in_specs=in_specs,
        out_specs=pl.BlockSpec((tokens, group * HD), lambda h: (0, first + h)),
        out_shape=jax.ShapeDtypeStruct((tokens, heads * HD), BF16),
        scratch_shapes=[
            pltpu.VMEM((keys_count, 2 * HD), BF16),
            pltpu.VMEM((tokens * parts, 2 * HD), BF16),
        ],
        input_output_aliases=aliases,
        compiler_params=params(1),
        cost_estimate=cost(8 * pairs * HD, 4 * count * keys_count * HD, pairs),
        name="attend",
    )(*operands)


def project_out(col_block, attended, weight, width, strips, kind, depth, at=0, add=None):
    rows = attended.shape[0]
    strip = rows // strips
    step = min(1024, width)
    steps = width // step

    def body(cols, x_ref, w_ref, *refs):
        total = jnp.dot(x_ref[...], w_ref[...], preferred_element_type=F32)
        if add is not None:
            total = total + refs[0][...]
        for i in range(strips):
            refs[i - strips][...] = total[i * strip : (i + 1) * strip].astype(kind)

    in_specs = [
        pl.BlockSpec((rows, depth), lambda n, cols: (0, at)),
        pl.BlockSpec((depth, step), lambda n, cols: (at, cols[0] * steps + n)),
    ]
    operands = [attended, weight]
    if add is not None:
        in_specs.append(pl.BlockSpec((rows, step), lambda n, cols: (0, n)))
        operands.append(add)
    return pl.pallas_call(
        body,
        grid_spec=pltpu.PrefetchScalarGridSpec(
            num_scalar_prefetch=1,
            grid=(steps,),
            in_specs=in_specs,
            out_specs=[pl.BlockSpec((strip, step), lambda n, cols: (0, n))] * strips,
        ),
        out_shape=[jax.ShapeDtypeStruct((strip, width), kind)] * strips,
        compiler_params=params(1),
        cost_estimate=cost(2 * rows * depth * width, depth * width * 2 + rows * width * 4),
        name="project_out",
    )(col_block, *operands)


def combine(own, parts, index, total_rows, out):
    rows, width = own.shape

    def body(*refs):
        total = refs[0][...]
        for ref in refs[1 : 1 + len(parts)]:
            total = total + ref[...].astype(F32)
        refs[-1][...] = total.astype(BF16)

    step = width
    in_specs = [pl.BlockSpec((rows, step), lambda n: (0, n))] * (1 + len(parts))
    operands = [own] + list(parts)
    aliases = {}
    if out is not None:
        aliases = {len(operands): 0}
        in_specs.append(pl.BlockSpec(memory_space=pl.ANY))
        operands.append(out)
    return pl.pallas_call(
        body,
        grid=(width // step,),
        in_specs=in_specs,
        out_specs=pl.BlockSpec((rows, step), lambda n: (index, n)),
        out_shape=jax.ShapeDtypeStruct((total_rows, width), BF16),
        input_output_aliases=aliases,
        compiler_params=params(1),
        cost_estimate=cost(0, rows * width * 8),
        name="combine",
    )(*operands)


def rotation(length, tokens):
    half = HD // 2
    freqs = jnp.exp(jnp.arange(half, dtype=F32) * (-2.0 * math.log(ROPE_BASE) / HD))
    positions = (length + jnp.arange(tokens, dtype=jnp.int32)).astype(F32)
    angles = positions[:, None] * freqs[None, :]
    cosine = jnp.cos(angles)
    sine = jnp.sin(angles)
    return jnp.concatenate([cosine, cosine], axis=1), jnp.concatenate([-sine, sine], axis=1)


def on_device(
    hidden, w_query, w_key, w_value, w_out, cache_keys, cache_values, cached_len, page_table
):
    tokens = hidden.shape[0]
    assert tokens == NEW
    seq = lax.axis_size("seq")
    tp = lax.axis_size("tp")
    query_heads = w_query.shape[1] // HD
    kv_heads = w_key.shape[1] // HD
    group = query_heads // kv_heads
    block_len = cache_keys.shape[1]
    per_peer = max(1, CTX // block_len // seq)
    request = lax.axis_index("seq")
    rank = lax.axis_index("tp")
    length = cached_len[request]

    span = per_peer * block_len
    split = [(0, kv_heads - 1), (kv_heads - 1, 1)] if kv_heads > 1 else [(0, 1)]
    own_row = jnp.reshape(rank, (1,)).astype(jnp.int32)
    rest_rows = jnp.stack([(rank - shift) % tp for shift in range(1, tp)]).astype(jnp.int32)
    cosine, sine = rotation(length, tokens)

    def pick(first, count):
        return pick_blocks(
            page_table, cached_len, cache_keys, cache_values, first, count, seq, per_peer
        )

    def exchange(block):
        return lax.all_to_all(block, "seq", 0, 0, tiled=True)

    def swap(x, shift):
        return lax.ppermute(x, "tp", [(i, (i + shift) % tp) for i in range(tp)])

    half_tokens = tokens // 2
    received = [exchange(pick(*split[0]))]
    arrivals = []
    for half in range(2):
        mine = hidden[half * half_tokens : (half + 1) * half_tokens]
        if arrivals:
            mine, arrivals[0][0] = lax.optimization_barrier((mine, arrivals[0][0]))
        arrivals.append([swap(mine, shift) for shift in range(1, tp)])
    own_parts = [project_own(own_row, hidden, w) for w in (w_key, w_value, w_query)]

    def rest(half, parts):
        def one(weight, part, scale):
            return project_rest(
                rest_rows, half, arrivals[half], weight, part, cosine, sine, scale
            )

        return [
            one(w_key, parts[0], 1.0),
            one(w_value, parts[1], None),
            one(w_query, parts[2], HD ** (-0.5) / math.log(2.0)),
        ]

    fresh = [rest(0, own_parts), rest(1, own_parts)]
    for first, count in split[1:]:
        block, received[-1], fresh = lax.optimization_barrier(
            (pick(first, count), received[-1], fresh)
        )
        received.append(exchange(block))
    bias = received[0][:, 2 * span * split[0][1], :span].astype(F32).reshape(1, seq * span)
    attended = [None, None]

    def run(first, count, half):
        piece = 0 if first < split[0][1] else 1
        attended[half] = attend(
            first,
            count,
            first - split[piece][0],
            group,
            fresh[half][2],
            [fresh[i][0] for i in range(half + 1)],
            [fresh[i][1] for i in range(half + 1)],
            received[piece],
            bias,
            attended[half],
        )

    width = w_out.shape[1] // tp
    targets = [jnp.reshape((rank + s) % tp, (1,)).astype(jnp.int32) for s in range(1, tp)]
    features = query_heads * HD
    per_head = group * HD
    early = per_head * split[0][1] if len(split) > 1 else features

    run(*split[0], 0)
    sums = []
    if len(split) > 1:
        sums = [project_out(t, attended[0], w_out, width, 1, F32, early)[0] for t in targets]
        received[1], attended, sums = lax.optimization_barrier(
            (received[1], attended, sums)
        )
        run(*split[1], 0)
        late = features - early
        other = [
            project_out(t, attended[0], w_out, width, 1, BF16, late, early // late, part)
            for t, part in zip(targets, sums)
        ]
    else:
        other = [project_out(t, attended[0], w_out, width, 1, BF16, features) for t in targets]
    other = [[swap(part[0], shift + 1)] for shift, part in enumerate(other)]
    run(*split[0], 1)
    if len(split) > 1:
        run(*split[1], 1)
    strips = 2 if tp == 2 else 1
    for shift, target in enumerate(targets):
        parts = project_out(target, attended[1], w_out, width, strips, BF16, features)
        other[shift] += [swap(part, shift + 1) for part in parts]
    if tp == 2:
        other[0][0], attended = lax.optimization_barrier((other[0][0], attended))
    own = project_out(own_row, attended[0], w_out, width, 1, F32, features)
    own += project_out(own_row, attended[1], w_out, width, strips, F32, features)
    out = None
    row = 0
    for i, part in enumerate(own):
        if i == len(own) - 1:
            total = part
            for arrived in other:
                total = total + arrived[i].astype(F32)
            return lax.dynamic_update_slice(out, total.astype(BF16), (row, 0))
        out = combine(part, [arrived[i] for arrived in other], row // part.shape[0], tokens, out)
        row += part.shape[0]
    return out


def solution(mesh):
    in_specs = (
        P("seq", "tp"),
        P(None, "tp"),
        P(None, "tp"),
        P(None, "tp"),
        P("tp", None),
        P("seq", None, "tp"),
        P("seq", None, "tp"),
        P(),
        P("seq", None),
    )
    out_specs = P("seq", "tp")
    return jax.shard_map(
        on_device, mesh=mesh, in_specs=in_specs, out_specs=out_specs, check_vma=False
    )
```

```python
import math

import jax
import jax.numpy as jnp
from jax import lax
from jax.experimental import pallas as pl
from jax.experimental.pallas import tpu as pltpu
from jax.sharding import PartitionSpec as P

HD = 128
NEW = 512
CTX = 2048
ROPE_BASE = 1000000.0
masked_score = -1e30
VMEM_LIMIT = 40 * 1024 * 1024
BF16 = jnp.bfloat16
F32 = jnp.float32


def params(count):
    return pltpu.CompilerParams(
        dimension_semantics=("arbitrary",) * count, vmem_limit_bytes=VMEM_LIMIT
    )


def cost(flops, moved, exps=0):
    return pl.CostEstimate(flops=flops, bytes_accessed=moved, transcendentals=exps)


def pick_blocks(page_table, cached_len, cache_keys, cache_values, first, count, seq, per_peer):
    masked = first == 0
    blocks, block_len, _ = cache_keys.shape
    span = per_peer * block_len
    rows = 2 * span * count + (8 if masked else 0)
    width = count * HD

    def body(table, lengths, keys, values, out, index):
        for slot in range(seq * per_peer):
            index[slot] = 0
        tally = seq * per_peer
        for r in range(seq):
            index[tally + r] = 0

        def place(b, carry):
            r = table[b, 0]
            taken = index[tally + r]
            index[r * per_peer + jnp.minimum(taken, per_peer - 1)] = b
            index[tally + r] = taken + 1
            return carry

        lax.fori_loop(0, blocks, place, 0)
        lane = lax.broadcasted_iota(jnp.int32, (8, HD), 1)
        for r in range(seq):
            mask = jnp.full((8, HD), masked_score, F32)
            for k in range(per_peer):
                b = index[r * per_peer + k]
                for h in range(count):
                    at = 2 * h * span + k * block_len
                    columns = slice(h * HD, (h + 1) * HD)
                    out[r, at : at + block_len, :] = keys[b, :, columns]
                    out[r, at + span : at + span + block_len, :] = values[b, :, columns]
                if masked:
                    filled = jnp.minimum(lengths[r] - table[b, 1] * block_len, block_len)
                    filled = jnp.where(index[tally + r] > k, filled, 0)
                    inside = (lane >= k * block_len) & (lane < k * block_len + filled)
                    mask = jnp.where(inside, 0.0, mask)
            if masked:
                out[r, 2 * span * count :, :] = mask.astype(BF16)

    part = pl.BlockSpec((blocks, block_len, width), lambda i: (0, 0, first // count))
    return pl.pallas_call(
        body,
        grid=(1,),
        in_specs=[
            pl.BlockSpec(memory_space=pltpu.SMEM),
            pl.BlockSpec(memory_space=pltpu.SMEM),
            part,
            part,
        ],
        out_specs=pl.BlockSpec((seq, rows, HD), lambda i: (0, 0, 0)),
        out_shape=jax.ShapeDtypeStruct((seq, rows, HD), BF16),
        scratch_shapes=[pltpu.SMEM((seq * per_peer + seq,), jnp.int32)],
        compiler_params=params(1),
        cost_estimate=cost(0, 2 * seq * rows * HD * 2),
        name="pick_blocks",
    )(page_table, cached_len, cache_keys, cache_values)


def project_own(row_block, x, weight):
    tokens, depth = x.shape
    width = weight.shape[1]
    step = min(512, width)

    def body(rows, x_ref, w_ref, o_ref):
        o_ref[...] = jnp.dot(x_ref[...], w_ref[...], preferred_element_type=F32)

    return pl.pallas_call(
        body,
        grid_spec=pltpu.PrefetchScalarGridSpec(
            num_scalar_prefetch=1,
            grid=(width // step,),
            in_specs=[
                pl.BlockSpec((tokens, depth), lambda n, rows: (0, 0)),
                pl.BlockSpec((depth, step), lambda n, rows: (rows[0], n)),
            ],
            out_specs=pl.BlockSpec((tokens, step), lambda n, rows: (0, n)),
        ),
        out_shape=jax.ShapeDtypeStruct((tokens, width), F32),
        compiler_params=params(1),
        cost_estimate=cost(2 * tokens * depth * width, depth * width * 2 + tokens * width * 4),
        name="project_own",
    )(row_block, x, weight)


def project_rest(row_blocks, half, pieces, weight, partial, cosine, sine, scale):
    tokens, depth = pieces[0].shape
    count = len(pieces)
    width = weight.shape[1]
    step = min(512, width)
    heads = step // HD

    def body(rows, *refs):
        x_refs = refs[:count]
        w_refs = refs[count : 2 * count]
        p_ref, c_ref, s_ref, o_ref = refs[2 * count :]
        total = p_ref[...]
        for x_ref, w_ref in zip(x_refs, w_refs):
            total = total + jnp.dot(x_ref[...], w_ref[...], preferred_element_type=F32)
        for h in range(heads):
            u = total[:, h * HD : (h + 1) * HD]
            if scale is not None:
                inverse = lax.rsqrt(jnp.mean(u * u, axis=-1, keepdims=True) + 1e-06) * scale
                u = u * inverse
                u = u * c_ref[...] + pltpu.roll(u, HD // 2, 1) * s_ref[...]
            o_ref[h] = u.astype(BF16)

    def weight_spec(i):
        return pl.BlockSpec((depth, step), lambda n, rows: (rows[i], n))

    return pl.pallas_call(
        body,
        grid_spec=pltpu.PrefetchScalarGridSpec(
            num_scalar_prefetch=1,
            grid=(width // step,),
            in_specs=[pl.BlockSpec((tokens, depth), lambda n, rows: (0, 0))] * count
            + [weight_spec(i) for i in range(count)]
            + [
                pl.BlockSpec((tokens, step), lambda n, rows: (half, n)),
                pl.BlockSpec((tokens, HD), lambda n, rows: (half, 0)),
                pl.BlockSpec((tokens, HD), lambda n, rows: (half, 0)),
            ],
            out_specs=pl.BlockSpec((heads, tokens, HD), lambda n, rows: (n, 0, 0)),
        ),
        out_shape=jax.ShapeDtypeStruct((width // HD, tokens, HD), BF16),
        compiler_params=params(1),
        cost_estimate=cost(
            2 * tokens * depth * count * width, depth * count * width * 2 + tokens * width * 8
        ),
        name="project_rest",
    )(row_blocks, *pieces, *([weight] * count), partial, cosine, sine)


def attend(first, count, at, group, queries, fresh_keys, fresh_values, cached, bias, attended):
    heads, tokens, _ = queries.shape
    parts = len(fresh_keys)
    sources = cached.shape[0]
    keys_count = bias.shape[1]
    rows = keys_count // sources
    tile = 128
    contract = (((1,), (1,)), ((), ()))

    def body(*refs):
        q_ref, c_ref, b_ref = refs[:3]
        key_refs = refs[3 : 3 + parts]
        value_refs = refs[3 + parts : 3 + 2 * parts]
        o_ref, old_values, new_values = refs[-3:]
        old_values[:, :HD] = c_ref[:, rows:].reshape(keys_count, HD)
        old_values[:, HD:] = jnp.ones((keys_count, HD), BF16)
        for i in range(parts):
            new_values[i * tokens : (i + 1) * tokens, :HD] = value_refs[i][0]
        new_values[:, HD:] = jnp.ones((tokens * parts, HD), BF16)
        cached_keys = c_ref[:, :rows].reshape(keys_count, HD)

        def product(q, keys):
            return lax.dot_general(q, keys, contract, preferred_element_type=F32)

        def scores(g, t):
            q = q_ref[g, t * tile : (t + 1) * tile]
            width = (t + 1) * tile
            out = [product(q, cached_keys) + b_ref[...]]
            out += [product(q, ref[0]) for ref in key_refs[:-1]]
            row = lax.broadcasted_iota(jnp.int32, (tile, width), 0) + t * tile
            col = lax.broadcasted_iota(jnp.int32, (tile, width), 1)
            out.append(jnp.where(col <= row, product(q, key_refs[-1][0, :width]), masked_score))
            return out

        work = [(g, t) for g in range(group) for t in range(tokens // tile)]
        ahead = scores(*work[0])
        for i, (g, t) in enumerate(work):
            now = ahead
            if i + 1 < len(work):
                ahead = scores(*work[i + 1])
            top = jnp.max(now[0], axis=1, keepdims=True)
            for part in now[1:]:
                top = jnp.maximum(top, jnp.max(part, axis=1, keepdims=True))
            now = [jnp.exp2(part - top).astype(BF16) for part in now]
            mixed = jnp.dot(now[0], old_values[...], preferred_element_type=F32)
            start = 0
            for part in now[1:]:
                values = new_values[start : start + part.shape[1]]
                mixed = mixed + jnp.dot(part, values, preferred_element_type=F32)
                start += part.shape[1]
            o_ref[t * tile : (t + 1) * tile, g * HD : (g + 1) * HD] = (
                mixed[:, :HD] / mixed[:, HD:]
            ).astype(BF16)

    head_spec = pl.BlockSpec((1, tokens, HD), lambda h: (first + h, 0, 0))
    in_specs = [
        pl.BlockSpec((group, tokens, HD), lambda h: (first + h, 0, 0)),
        pl.BlockSpec((sources, 2 * rows, HD), lambda h: (0, at + h, 0)),
        pl.BlockSpec((1, keys_count), lambda h: (0, 0)),
    ] + [head_spec] * (2 * parts)
    operands = [queries, cached, bias] + list(fresh_keys) + list(fresh_values)
    aliases = {}
    if attended is not None:
        aliases = {len(operands): 0}
        in_specs.append(pl.BlockSpec(memory_space=pl.ANY))
        operands.append(attended)
    pairs = count * group * tokens * (keys_count + tokens * parts)
    return pl.pallas_call(
        body,
        grid=(count,),
        in_specs=in_specs,
        out_specs=pl.BlockSpec((tokens, group * HD), lambda h: (0, first + h)),
        out_shape=jax.ShapeDtypeStruct((tokens, heads * HD), BF16),
        scratch_shapes=[
            pltpu.VMEM((keys_count, 2 * HD), BF16),
            pltpu.VMEM((tokens * parts, 2 * HD), BF16),
        ],
        input_output_aliases=aliases,
        compiler_params=params(1),
        cost_estimate=cost(8 * pairs * HD, 4 * count * keys_count * HD, pairs),
        name="attend",
    )(*operands)


def project_out(col_block, attended, weight, width, strips, kind, depth, at=0, add=None):
    rows = attended.shape[0]
    strip = rows // strips
    step = min(1024 if depth > 512 else 512, width)
    steps = width // step

    def body(cols, x_ref, w_ref, *refs):
        total = jnp.dot(x_ref[...], w_ref[...], preferred_element_type=F32)
        if add is not None:
            total = total + refs[0][...]
        for i in range(strips):
            refs[i - strips][...] = total[i * strip : (i + 1) * strip].astype(kind)

    in_specs = [
        pl.BlockSpec((rows, depth), lambda n, cols: (0, at)),
        pl.BlockSpec((depth, step), lambda n, cols: (at, cols[0] * steps + n)),
    ]
    operands = [attended, weight]
    if add is not None:
        in_specs.append(pl.BlockSpec((rows, step), lambda n, cols: (0, n)))
        operands.append(add)
    return pl.pallas_call(
        body,
        grid_spec=pltpu.PrefetchScalarGridSpec(
            num_scalar_prefetch=1,
            grid=(steps,),
            in_specs=in_specs,
            out_specs=[pl.BlockSpec((strip, step), lambda n, cols: (0, n))] * strips,
        ),
        out_shape=[jax.ShapeDtypeStruct((strip, width), kind)] * strips,
        compiler_params=params(1),
        cost_estimate=cost(2 * rows * depth * width, depth * width * 2 + rows * width * 4),
        name="project_out",
    )(col_block, *operands)


def combine(own, parts, index, total_rows, out):
    rows, width = own.shape

    def body(*refs):
        total = refs[0][...]
        for ref in refs[1 : 1 + len(parts)]:
            total = total + ref[...].astype(F32)
        refs[-1][...] = total.astype(BF16)

    step = width
    in_specs = [pl.BlockSpec((rows, step), lambda n: (0, n))] * (1 + len(parts))
    operands = [own] + list(parts)
    aliases = {}
    if out is not None:
        aliases = {len(operands): 0}
        in_specs.append(pl.BlockSpec(memory_space=pl.ANY))
        operands.append(out)
    return pl.pallas_call(
        body,
        grid=(width // step,),
        in_specs=in_specs,
        out_specs=pl.BlockSpec((rows, step), lambda n: (index, n)),
        out_shape=jax.ShapeDtypeStruct((total_rows, width), BF16),
        input_output_aliases=aliases,
        compiler_params=params(1),
        cost_estimate=cost(0, rows * width * 8),
        name="combine",
    )(*operands)


def rotation(length, tokens):
    half = HD // 2
    freqs = jnp.exp(jnp.arange(half, dtype=F32) * (-2.0 * math.log(ROPE_BASE) / HD))
    positions = (length + jnp.arange(tokens, dtype=jnp.int32)).astype(F32)
    angles = positions[:, None] * freqs[None, :]
    cosine = jnp.cos(angles)
    sine = jnp.sin(angles)
    return jnp.concatenate([cosine, cosine], axis=1), jnp.concatenate([-sine, sine], axis=1)


def on_device(
    hidden, w_query, w_key, w_value, w_out, cache_keys, cache_values, cached_len, page_table
):
    tokens = hidden.shape[0]
    assert tokens == NEW
    seq = lax.axis_size("seq")
    tp = lax.axis_size("tp")
    query_heads = w_query.shape[1] // HD
    kv_heads = w_key.shape[1] // HD
    group = query_heads // kv_heads
    block_len = cache_keys.shape[1]
    per_peer = max(1, CTX // block_len // seq)
    request = lax.axis_index("seq")
    rank = lax.axis_index("tp")
    length = cached_len[request]

    span = per_peer * block_len
    split = [(0, kv_heads - 1), (kv_heads - 1, 1)] if kv_heads > 1 else [(0, 1)]
    own_row = jnp.reshape(rank, (1,)).astype(jnp.int32)
    rest_rows = jnp.stack([(rank - shift) % tp for shift in range(1, tp)]).astype(jnp.int32)
    cosine, sine = rotation(length, tokens)

    def pick(first, count):
        return pick_blocks(
            page_table, cached_len, cache_keys, cache_values, first, count, seq, per_peer
        )

    def exchange(block):
        return lax.all_to_all(block, "seq", 0, 0, tiled=True)

    def swap(x, shift):
        return lax.ppermute(x, "tp", [(i, (i + shift) % tp) for i in range(tp)])

    half_tokens = tokens // 2
    received = [exchange(pick(*split[0]))]
    arrivals = []
    for half in range(2):
        mine = hidden[half * half_tokens : (half + 1) * half_tokens]
        if arrivals:
            mine, arrivals[0][0] = lax.optimization_barrier((mine, arrivals[0][0]))
        arrivals.append([swap(mine, shift) for shift in range(1, tp)])
    own_parts = [project_own(own_row, hidden, w) for w in (w_key, w_value, w_query)]

    def rest(half, parts):
        def one(weight, part, scale):
            return project_rest(
                rest_rows, half, arrivals[half], weight, part, cosine, sine, scale
            )

        return [
            one(w_key, parts[0], 1.0),
            one(w_value, parts[1], None),
            one(w_query, parts[2], HD ** (-0.5) / math.log(2.0)),
        ]

    fresh = [rest(0, own_parts), rest(1, own_parts)]
    for first, count in split[1:]:
        block, received[-1], fresh = lax.optimization_barrier(
            (pick(first, count), received[-1], fresh)
        )
        received.append(exchange(block))
    bias = received[0][:, 2 * span * split[0][1], :span].astype(F32).reshape(1, seq * span)
    attended = [None, None]

    def run(first, count, half):
        piece = 0 if first < split[0][1] else 1
        attended[half] = attend(
            first,
            count,
            first - split[piece][0],
            group,
            fresh[half][2],
            [fresh[i][0] for i in range(half + 1)],
            [fresh[i][1] for i in range(half + 1)],
            received[piece],
            bias,
            attended[half],
        )

    width = w_out.shape[1] // tp
    targets = [jnp.reshape((rank + s) % tp, (1,)).astype(jnp.int32) for s in range(1, tp)]
    features = query_heads * HD
    per_head = group * HD
    early = per_head * split[0][1] if len(split) > 1 else features

    run(*split[0], 0)
    sums = []
    if len(split) > 1:
        sums = [project_out(t, attended[0], w_out, width, 1, F32, early)[0] for t in targets]
        received[1], attended, sums = lax.optimization_barrier(
            (received[1], attended, sums)
        )
        run(*split[1], 0)
        late = features - early
        other = [
            project_out(t, attended[0], w_out, width, 1, BF16, late, early // late, part)
            for t, part in zip(targets, sums)
        ]
    else:
        other = [project_out(t, attended[0], w_out, width, 1, BF16, features) for t in targets]
    other = [[swap(part[0], shift + 1)] for shift, part in enumerate(other)]
    run(*split[0], 1)
    if len(split) > 1:
        run(*split[1], 1)
    strips = 2 if tp == 2 else 1
    for shift, target in enumerate(targets):
        parts = project_out(target, attended[1], w_out, width, strips, BF16, features)
        other[shift] += [swap(part, shift + 1) for part in parts]
    if tp == 2:
        other[0][0], attended = lax.optimization_barrier((other[0][0], attended))
    own = project_out(own_row, attended[0], w_out, width, 1, F32, features)
    own += project_out(own_row, attended[1], w_out, width, strips, F32, features)
    out = None
    row = 0
    for i, part in enumerate(own):
        if i == len(own) - 1:
            total = part
            for arrived in other:
                total = total + arrived[i].astype(F32)
            return lax.dynamic_update_slice(out, total.astype(BF16), (row, 0))
        out = combine(part, [arrived[i] for arrived in other], row // part.shape[0], tokens, out)
        row += part.shape[0]
    return out


def solution(mesh):
    in_specs = (
        P("seq", "tp"),
        P(None, "tp"),
        P(None, "tp"),
        P(None, "tp"),
        P("tp", None),
        P("seq", None, "tp"),
        P("seq", None, "tp"),
        P(),
        P("seq", None),
    )
    out_specs = P("seq", "tp")
    return jax.shard_map(
        on_device, mesh=mesh, in_specs=in_specs, out_specs=out_specs, check_vma=False
    )
```
